32 devices in a mesh: grp: 2 (over x), col: 16 (over z, y, core).
Axes of the slice: x: 2, y: 2, z: 4, core: 2. Of those that a mesh axis runs over, the one named last changes fastest.
Arguments:
- state_emb: bfloat16 [8192, 512], P('col'), may hold values from -6 to 6
- from_weight: bfloat16 [512, 512], replicated, may hold values from -0.25 to 0.25
- to_weight: bfloat16 [512, 512], replicated, may hold values from -0.25 to 0.25
- emit_weight: bfloat16 [512, 512], replicated, may hold values from -0.25 to 0.25
- code_emb: bfloat16 [4096, 512], replicated, may hold values from -0.25 to 0.25
- init_vec: bfloat16 [512], replicated, may hold values from -0.25 to 0.25
- restart_logit: float32 [8192], P('col'), may hold values from -3 to 0
- block_mask: int32 [16, 8], replicated, may hold values from 0 to 1, as said below
- codes: int32 [64, 4], P('grp'), parts along dimension 0, may hold values from 0 to 4095
- lengths: int32 [64], P('grp'), parts along dimension 0, may hold values from 1 to 4, as said below
Outputs:
- scaled: float32 [64, 8192], P('grp', 'col'), parts along dimension 0
- log_like: float32 [64], P('grp'), parts along dimension 0
The draws below stay inside these ranges and needn't reach their ends.
There are 2 independent parts, one for each index of `grp`. The reference program is written for one: setup_inputs(seed, part) draws one part's arguments, and reference() takes and returns one part's arrays. A program takes and returns all parts, laid end to end along the dimension named above; an argument that names none is the same for every part. Nothing has to cross between parts.
Inputs may be any that keep to these rules, and one draw needn't show every extreme that they name: `block_mask`: entries are 0 or 1, and entry [c, c % 8] is 1 for every block c. `lengths`: some sequence has length 4 and another has length 1.
All inputs are finite; a program needn't handle non-finite values.
Results may differ from the reference program's by a relative error of at most 0.0057.
Values may be sent and summed in bfloat16 or wider, within the bound.
No kernel may reach another device: no remote copies, remote signals or barrier semaphores. Data moves between devices by JAX's collectives and lax.ppermute only.
A program may use at most 128 MiB of HBM per device.

```python
import math
import jax
import jax.numpy as jnp
import numpy as np
from jax import lax

EMBED = 512
VOCAB = 4096
STATE_DEV = 512
CLUSTER = 8
BATCH = 32
STEPS = 4
STATES = 8192
N_COL = 16


def draw_block_mask(key, part):
    random_bits = jax.random.randint(key, (N_COL, CLUSTER), 0, 2)
    own_place = (jnp.arange(N_COL) % CLUSTER)[:, None] == jnp.arange(CLUSTER)[None, :]
    return jnp.where(own_place, 1, random_bits).astype(jnp.int32)


def draw_lengths(key, part):
    drawn = jax.random.randint(jax.random.fold_in(key, 11), (BATCH,), 1, STEPS + 1)
    order = jax.random.permutation(jax.random.fold_in(key, 23), BATCH)
    longest = order[0]
    shortest = order[1]
    return drawn.at[longest].set(STEPS).at[shortest].set(1).astype(jnp.int32)


def plant(values, stream_key, smallest, top_value):
    shape = values.shape
    index_at = [jax.random.randint(jax.random.fold_in(stream_key, axis), (), 0, shape[axis]) for axis in range(len(shape))]
    values = values.at[tuple(index_at)].set(smallest)
    longest = shape.index(max(shape))
    index_at[longest] = (index_at[longest] + 1) % shape[longest]
    return values.at[tuple(index_at)].set(top_value)


def shard_levels(key, dims, shards, low, largest):
    def one(dim, shards_of):
        draws = jax.random.uniform(jax.random.fold_in(jax.random.fold_in(key, 6), dim), (shards_of,), jnp.float32, low / len(shards), largest / len(shards))
        return jnp.repeat(jnp.exp(draws), dims[dim] // shards_of).reshape((-1,) + (1,) * (len(dims) - dim - 1))

    gain = one(*shards[0])
    for cut in shards[1:]:
        gain = gain * one(*cut)
    return gain


def rank_table(amount, skew):
    weights = [(1 << 20) // math.isqrt(rank ** skew) + 1 for rank in range(1, amount + 1)]
    spread = 1 + sum(weights) // (1 << 30)
    return np.cumsum(np.array([max(1, weight // spread) for weight in weights]))


def skewed_ids(stream_key, shape, count, skew):
    table = rank_table(count, skew)
    pick = jax.random.randint(jax.random.fold_in(stream_key, 1), shape, 0, int(table[count - 1]))
    standing = jnp.searchsorted(jnp.asarray(table, jnp.int32), pick, side="right")
    return jax.random.permutation(jax.random.fold_in(stream_key, 2), count)[standing].astype(jnp.int32)


def noise(own_key, extent, spread, bound, cuts=(), kind=jnp.bfloat16):
    result = spread * jax.random.normal(own_key, extent, jnp.float32)
    if cuts:
        result = result * shard_levels(own_key, extent, cuts, -0.22, 0.18)
    return jnp.clip(result, -bound, bound).astype(kind)


def setup_inputs(seed: int = 0, part: int = 0) -> dict:
    arg_keys = jax.random.split(jax.random.key(seed), 11)
    own_keys = jax.random.split(jax.random.fold_in(arg_keys[10], part), 11)
    state_emb = noise(arg_keys[0], (STATES, EMBED), 1.0, 6.0, ((0, 16),))
    from_weight = noise(arg_keys[1], (EMBED, EMBED), EMBED ** -0.5, 0.25)
    to_weight = noise(arg_keys[2], (EMBED, EMBED), EMBED ** -0.5, 0.25)
    emit_weight = noise(arg_keys[3], (EMBED, EMBED), EMBED ** -0.5, 0.25)
    code_emb = noise(arg_keys[4], (VOCAB, EMBED), EMBED ** -0.5, 0.25)
    init_vec = noise(arg_keys[5], (EMBED,), EMBED ** -0.5, 0.25)
    restart_logit = jnp.clip(-3.0 + 3.0 * jax.random.uniform(arg_keys[6], (STATES,), jnp.float32) ** shard_levels(arg_keys[6], (STATES,), ((0, 16),), -0.2, 0.2), -3.0, 0.0)
    block_mask = draw_block_mask(jax.random.fold_in(arg_keys[10], 71), part)
    codes = plant(skewed_ids(own_keys[8], (BATCH, STEPS), VOCAB, 2), jax.random.fold_in(own_keys[8], 3), 0, VOCAB - 1).astype(jnp.int32)
    lengths = draw_lengths(jax.random.fold_in(jax.random.fold_in(arg_keys[10], part), 71), part)
    return dict(state_emb=state_emb, from_weight=from_weight, to_weight=to_weight, emit_weight=emit_weight, code_emb=code_emb, init_vec=init_vec, restart_logit=restart_logit, block_mask=block_mask, codes=codes, lengths=lengths)


SOFT_CAP = 10.0


def soft_cap(values):
    return SOFT_CAP * jnp.tanh(values / SOFT_CAP)


def reference(state_emb, from_weight, to_weight, emit_weight, code_emb, init_vec, restart_logit, block_mask, codes, lengths):
    from_part = jnp.dot(state_emb, from_weight, preferred_element_type=jnp.float32).astype(jnp.bfloat16)
    to_part = jnp.dot(state_emb, to_weight, preferred_element_type=jnp.float32).astype(jnp.bfloat16)
    query_part = jnp.dot(state_emb, emit_weight, preferred_element_type=jnp.float32).astype(jnp.bfloat16)
    cluster_states = CLUSTER * STATE_DEV
    clusters = N_COL // CLUSTER
    logit_scale = 2.0 / (EMBED ** 0.5)

    def transitions(cluster_id):
        start_row = (cluster_id * cluster_states).astype(jnp.int32)
        rows_from = lax.dynamic_slice_in_dim(from_part, start_row, cluster_states, 0)
        rows_to = lax.dynamic_slice_in_dim(to_part, start_row, cluster_states, 0)
        logits = jnp.dot(rows_from, rows_to.T, preferred_element_type=jnp.float32) * logit_scale
        allowed_blocks = lax.dynamic_slice_in_dim(block_mask, (cluster_id * CLUSTER).astype(jnp.int32), CLUSTER, 0)
        allowed = jnp.repeat(jnp.repeat(allowed_blocks.T, STATE_DEV, axis=0), STATE_DEV, axis=1) == 1
        weights_exp = jnp.where(allowed, jnp.exp(soft_cap(logits)), jnp.zeros_like(logits))
        row_sum = jnp.sum(weights_exp, axis=1)
        return (weights_exp / row_sum[:, None]).astype(jnp.bfloat16)

    trans_blocks = lax.map(transitions, jnp.arange(clusters, dtype=jnp.int32))
    flat_codes = codes.reshape(-1)

    def emit_block(block_id):
        query_block = lax.dynamic_slice_in_dim(query_part, (block_id * STATE_DEV).astype(jnp.int32), STATE_DEV, 0)
        emit_full = jnp.exp(soft_cap(3.0 * jnp.dot(query_block, code_emb.T, preferred_element_type=jnp.float32)))
        emit_total = jnp.sum(emit_full, axis=1)
        return jnp.take(emit_full, flat_codes, axis=1) / emit_total[:, None]

    picked = lax.map(emit_block, jnp.arange(N_COL, dtype=jnp.int32))
    emission = picked.reshape(STATES, BATCH, STEPS).transpose(2, 1, 0)
    prior_raw = jnp.exp(soft_cap(2.0 * jnp.dot(state_emb, init_vec, preferred_element_type=jnp.float32)))
    prior = prior_raw / jnp.sum(prior_raw)
    restart_prob = jax.nn.sigmoid(restart_logit)
    forward = prior[None, :] * emission[0]
    totals = jnp.sum(forward, axis=1)
    scaled = forward / totals[:, None]
    log_like = jnp.log(totals)

    def block_product(pair):
        return jnp.dot(pair[0], pair[1], preferred_element_type=jnp.float32)

    for step_num in range(1, STEPS):
        weighted = (scaled * (1.0 - restart_prob)[None, :]).astype(jnp.bfloat16)
        restart = jnp.sum(scaled * restart_prob[None, :], axis=1)
        grouped = weighted.reshape(BATCH, clusters, cluster_states).transpose(1, 0, 2)
        moved = lax.map(block_product, (grouped, trans_blocks))
        predicted = moved.transpose(1, 0, 2).reshape(BATCH, STATES) + prior[None, :] * restart[:, None]
        forward = predicted * emission[step_num]
        totals = jnp.sum(forward, axis=1)
        is_live = step_num < lengths
        scaled = jnp.where(is_live[:, None], forward / totals[:, None], scaled)
        log_like = log_like + jnp.where(is_live, jnp.log(totals), jnp.zeros_like(totals))
    return scaled, log_like
```

```python
import math

import jax
import jax.numpy as jnp
from jax import lax
from jax.experimental import pallas as pl
from jax.experimental.pallas import tpu as pltpu
from jax.sharding import PartitionSpec as P

SOFT_CAP = 10.0
EMIT_SCALE = 2.0**20
F32 = jnp.float32
BF16 = jnp.bfloat16
NT = (((1,), (1,)), ((), ()))
NN = (((1,), (0,)), ((), ()))


def soft_cap(values):
    return SOFT_CAP * jnp.tanh(values * (1.0 / SOFT_CAP))


def dot(lhs, rhs, dims):
    return lax.dot_general(lhs, rhs, dims, preferred_element_type=F32)


def across(shard, apart, axis="col"):
    return lax.ppermute(shard, axis, [(i, i ^ apart) for i in range(lax.axis_size(axis))])


def vmem_call(body, out_shape, name, flops=0, nbytes=0, n_in=None, smem=()):
    def run(*args):
        in_specs = [
            pl.BlockSpec(memory_space=pltpu.SMEM if k in smem else pltpu.VMEM)
            for k in range(len(args))
        ]
        outs = jax.tree.map(lambda s: pl.BlockSpec(memory_space=pltpu.VMEM), out_shape)
        return pl.pallas_call(
            body,
            out_shape=out_shape,
            in_specs=in_specs,
            out_specs=outs,
            name=name,
            cost_estimate=pl.CostEstimate(flops=flops, bytes_accessed=nbytes, transcendentals=0),
            compiler_params=pltpu.CompilerParams(vmem_limit_bytes=40 << 20),
        )(*args)

    return run


def shape(dims, dtype):
    return jax.ShapeDtypeStruct(dims, dtype)


def project_kernel(emb, weight, out):
    out[...] = dot(emb[...], weight[...], NN).astype(BF16)


def sources_kernel(emb, from_w, emit_w, init_vec, from_out, query_out, prior_out):
    from_out[...] = dot(emb[...], from_w[...], NN).astype(BF16)
    query_out[...] = dot(emb[...], emit_w[...], NN).astype(BF16)
    prior = dot(jnp.broadcast_to(init_vec[...], (8, emb.shape[1])), emb[...], NT)
    prior_out[...] = jnp.exp(soft_cap(2.0 * prior))[:1]


def emission_kernel(half_tiles, place, code, query, codes, pick_out, total_out, rows_acc, total_acc):
    tile = pl.program_id(0)
    tile_rows = code.shape[0]

    @pl.when(tile == 0)
    def _():
        rows_acc[...] = jnp.zeros_like(rows_acc)
        total_acc[...] = jnp.zeros_like(total_acc)

    ids = codes[...]
    lanes = lax.broadcasted_iota(jnp.int32, (ids.shape[0], tile_rows), 1) + tile * tile_rows
    one_hot = jnp.where(lanes == ids, 1.0, 0.0).astype(BF16)
    rows_acc[...] += dot(one_hot, code[...], NN)

    @pl.when(tile // half_tiles == place[0])
    def _():
        def chunk(k, carry):
            rows = code[pl.ds(pl.multiple_of(k * 128, 128), 128), :]
            logits = dot(rows, query[...], NT)
            weights = jnp.exp(soft_cap(3.0 * logits))
            return carry + jnp.sum(weights.reshape(16, 8, -1), axis=0)

        total_acc[...] += lax.fori_loop(
            0, tile_rows // 128, chunk, jnp.zeros(total_acc.shape, F32), unroll=True
        )

    @pl.when(tile == pl.num_programs(0) - 1)
    def _():
        pick_out[...] = jnp.exp(soft_cap(3.0 * dot(rows_acc[...].astype(BF16), query[...], NT)))
        total_out[...] = jnp.sum(total_acc[...], axis=0, keepdims=True)


def lane_pack(columns, rows):
    lane = lax.broadcasted_iota(jnp.int32, (rows, 128), 1)
    packed = jnp.zeros((rows, 128), F32)
    for k, column in enumerate(columns):
        packed = jnp.where(lane == k, column, packed)
    return packed


def lane_pick(packed, k):
    lane = lax.broadcasted_iota(jnp.int32, packed.shape, 1)
    return jnp.sum(jnp.where(lane == k, packed, 0.0), axis=1, keepdims=True)


def hidden_kernel(pick, total_a, total_b, prior, logit, emit_out, msg_out):
    batch = pick.shape[0] // 4
    factor = EMIT_SCALE / (total_a[...] + total_b[...])
    emit = pick[...] * factor
    emit_out[...] = emit
    p = prior[...]
    restart = jax.nn.sigmoid(logit[...])
    first = p * emit[:batch]
    third = p * emit[2 * batch : 3 * batch]
    states = p.shape[1]
    msg_out[:batch, :states] = first * (1.0 - restart)
    msg_out[batch:, :states] = third * (1.0 - restart)
    mass = jnp.sum(first * restart, axis=1, keepdims=True)
    norm = jnp.broadcast_to(jnp.sum(p, axis=1, keepdims=True), mass.shape)
    msg_out[:batch, states:] = lane_pack([mass, norm], batch)
    msg_out[batch:, states:] = jnp.zeros((batch, 128), F32)


def weights_kernel(scale, to_blk, from_a, from_b, allow, wt_out, sum_out):
    states = from_a.shape[0]
    for side, source in ((0, from_a), (1, from_b)):
        keep = allow[side]

        def chunk(k, carry):
            rows = pl.ds(pl.multiple_of(k * 128, 128), 128)
            logits = dot(to_blk[rows, :], source[...], NT) * scale
            weights = jnp.exp(soft_cap(logits)) * keep
            wt_out[rows, side * states : (side + 1) * states] = weights.astype(BF16)
            return carry + jnp.sum(weights.reshape(16, 8, -1), axis=0)

        sums = lax.fori_loop(
            0, to_blk.shape[0] // 128, chunk, jnp.zeros((8, states), F32), unroll=True
        )
        sum_out[:, side * states : (side + 1) * states] = jnp.sum(sums, axis=0, keepdims=True)


def first_kernel(msg_a, msg_b, sums_own, sums_sib, mass, w0, w1, w2, w3, own, s1, s2, s3, inv_out):
    states = w0.shape[0]
    batch = mass.shape[0]
    rho_a = sums_own[:, :states] + sums_sib[:, states:]
    rho_b = sums_own[:, states:] + sums_sib[:, :states]
    inv_a = 1.0 / rho_a
    inv_out[...] = inv_a
    u_a = (msg_a[:, :states] * inv_a).astype(BF16)
    u_b = (msg_b[:, :states] * (1.0 / rho_b)).astype(BF16)
    u = jnp.concatenate([u_a, u_b], axis=1)
    own[...] = dot(u, w0[...], NT)
    total = mass[...]
    high = total.astype(BF16)
    low = (total - high.astype(F32)).astype(BF16)
    for w, s in ((w1, s1), (w2, s2), (w3, s3)):
        s[:, :states] = dot(u, w[...], NT).astype(BF16)
        s[:batch, states:] = high
        s[batch:, states:] = low


def combine_first_kernel(
    own, r1, r2, r3, mass, emit, prior, logit, inv, f_out, chain_out, u_out, part_out
):
    states = own.shape[1]
    batch = mass.shape[0]
    summed = own[...]
    total = mass[...]
    for r in (r1, r2, r3):
        summed = summed + r[:, :states].astype(F32)
        total = total + r[:batch, states:].astype(F32) + r[batch:, states:].astype(F32)
    ratio = lane_pick(total, 0) / lane_pick(total, 1)
    p = prior[...]
    restart = jax.nn.sigmoid(logit[...])
    f = emit[batch : 2 * batch] * (summed[:batch] + p * ratio)
    f_out[...] = f
    chain_out[...] = emit[3 * batch :] * summed[batch:]
    u_out[...] = (f * (1.0 - restart) * inv[...]).astype(BF16)
    part_out[...] = lane_pack(
        [lane_pick(total, 1), jnp.sum(f * restart, axis=1, keepdims=True)], batch
    )


def step_kernel(u_a, u_b, w0, w1, w2, w3, own, s1, s2, s3):
    u = jnp.concatenate([u_a[...], u_b[...]], axis=1)
    own[...] = dot(u, w0[...], NT)
    for w, s in ((w1, s1), (w2, s2), (w3, s3)):
        s[...] = dot(u, w[...], NT).astype(BF16)


def combine_kernel(own, r1, r2, r3, emit, logit, inv, g_out, u_out):
    batch = own.shape[0]
    summed = own[...]
    for r in (r1, r2, r3):
        summed = summed + r[...].astype(F32)
    restart = jax.nn.sigmoid(logit[...])
    g = emit[2 * batch : 3 * batch] * summed
    g_out[...] = g
    u_out[...] = (g * (1.0 - restart) * inv[...]).astype(BF16)


def last_kernel(
    own, r1, r2, r3, emit, prior, logit, f1, g2, chain, part, lengths, main_out, part_out
):
    batch = own.shape[0]
    summed = own[...]
    for r in (r1, r2, r3):
        summed = summed + r[...].astype(F32)
    restart = jax.nn.sigmoid(logit[...])
    p = prior[...]
    e = emit[...]
    length = lengths[...]
    h2 = p * e[2 * batch : 3 * batch]
    h3 = p * e[3 * batch :]
    main = jnp.where(
        length == 1,
        p * e[:batch],
        jnp.where(
            length == 2, f1[...], jnp.where(length == 3, g2[...], e[3 * batch :] * summed)
        ),
    )
    side = jnp.where(length == 3, h2, jnp.where(length == 4, chain[...], 0.0))
    tail = jnp.where(length == 4, h3, 0.0)
    main_out[0] = main
    main_out[1] = side
    main_out[2] = tail

    def row(values):
        return jnp.sum(values, axis=1, keepdims=True)

    part_out[...] = lane_pack(
        [
            lane_pick(part[...], 1),
            row(g2[...] * restart),
            row(h2 * restart),
            row(main),
            row(side),
            row(tail),
        ],
        batch,
    )


def finish_kernel(main, part, norm, lengths, scaled_out, like_out):
    total = part[...]
    z = lane_pick(norm[...], 0)
    mass1 = lane_pick(total, 0) / z
    mass2 = (lane_pick(total, 1) + mass1 * lane_pick(total, 2)) / z
    full = lane_pick(total, 3) + mass1 * lane_pick(total, 4) + mass2 * lane_pick(total, 5)
    values = main[0] + mass1 * main[1] + mass2 * main[2]
    scaled_out[...] = values / full
    steps = lengths[...].astype(F32)
    like = jnp.log(full) - jnp.log(z) - steps * math.log(EMIT_SCALE)
    like_out[...] = jnp.broadcast_to(like, like_out.shape)


def per_device(
    state_emb,
    from_weight,
    to_weight,
    emit_weight,
    code_emb,
    init_vec,
    restart_logit,
    block_mask,
    codes,
    lengths,
):
    states, width = state_emb.shape
    vocab = code_emb.shape[0]
    cluster = block_mask.shape[1]
    batch, steps = codes.shape
    cols = lax.axis_size("col")
    parts = lax.axis_size("grp")
    dev = lax.axis_index("col")
    place = dev % cluster
    logit = restart_logit.reshape(1, states)
    length_col = lengths.reshape(batch, 1)

    to_own = vmem_call(project_kernel, shape((states, width), BF16), "to_part")(
        state_emb, to_weight
    )
    to_y = across(to_own, 2)
    to_z = across(to_own, 4)

    from_own, query, prior = vmem_call(
        sources_kernel,
        (
            shape((states, width), BF16),
            shape((states, width), BF16),
            shape((1, states), F32),
        ),
        "sources",
    )(state_emb, from_weight, emit_weight, init_vec.reshape(1, width))
    from_sib = across(from_own, 1)

    tile = 512
    tiles = vocab // tile
    flat_codes = codes.T.reshape(batch * steps, 1)
    pick, total = pl.pallas_call(
        lambda *refs: emission_kernel(tiles // parts, *refs),
        out_shape=(shape((batch * steps, states), F32), shape((1, states), F32)),
        grid_spec=pltpu.PrefetchScalarGridSpec(
            num_scalar_prefetch=1,
            grid=(tiles,),
            in_specs=[
                pl.BlockSpec((tile, width), lambda k, place: (k, 0)),
                pl.BlockSpec((states, width), lambda k, place: (0, 0)),
                pl.BlockSpec((batch * steps, 1), lambda k, place: (0, 0)),
            ],
            out_specs=(
                pl.BlockSpec((batch * steps, states), lambda k, place: (0, 0)),
                pl.BlockSpec((1, states), lambda k, place: (0, 0)),
            ),
            scratch_shapes=[
                pltpu.VMEM((batch * steps, width), F32),
                pltpu.VMEM((8, states), F32),
            ],
        ),
        name="emission",
        compiler_params=pltpu.CompilerParams(vmem_limit_bytes=40 << 20),
    )(lax.axis_index("grp").reshape(1), code_emb, query, flat_codes)
    total_other = across(total, 1, "grp")

    emit, msg = vmem_call(
        hidden_kernel,
        (shape((batch * steps, states), F32), shape((2 * batch, states + 128), F32)),
        "hidden",
    )(pick, total, total_other, prior, logit)
    msg_sib = across(msg, 1)
    mass = msg[:batch, states:] + msg_sib[:batch, states:]
    apart = cluster
    while apart < cols:
        mass = mass + across(mass, apart)
        apart *= 2

    half = states // 2
    to_d0 = across(to_z[:half], 2)
    to_d1 = across(to_y[half:], 4)
    to_d = jnp.concatenate([to_d0, to_d1], axis=0)

    scale = 2.0 / math.sqrt(width)
    row_sums = None
    wts = []
    for k, block in enumerate((to_own, to_y, to_z, to_d)):
        allow = lax.dynamic_slice(block_mask, (dev ^ (2 * k), 0), (1, cluster))[0]
        pair = jnp.stack([allow[place], allow[place ^ 1]]).astype(F32)
        wt, sums = vmem_call(
            lambda *refs: weights_kernel(scale, *refs),
            (shape((states, 2 * states), BF16), shape((1, 2 * states), F32)),
            "weights",
            smem=(3,),
        )(block, from_own, from_sib, pair)
        wts.append(wt)
        row_sums = sums if row_sums is None else row_sums + sums
    row_sums_sib = across(row_sums, 1)

    out = vmem_call(
        first_kernel,
        (shape((2 * batch, states), F32),)
        + (shape((2 * batch, states + 128), BF16),) * 3
        + (shape((1, states), F32),),
        "first",
    )(msg, msg_sib, row_sums, row_sums_sib, mass, *wts)
    own, sends, inv = out[0], out[1:4], out[4]
    received = [across(s, 2 * (k + 1)) for k, s in enumerate(sends)]
    f1, chain, u1, part = vmem_call(
        combine_first_kernel,
        (
            shape((batch, states), F32),
            shape((batch, states), F32),
            shape((batch, states), BF16),
            shape((batch, 128), F32),
        ),
        "combine_first",
    )(own, *received, mass, emit, prior, logit, inv)

    def step(u):
        u_sib = across(u, 1)
        own, *sends = vmem_call(
            step_kernel,
            (shape((batch, states), F32),) + (shape((batch, states), BF16),) * 3,
            "step",
        )(u, u_sib, *wts)
        return [own] + [across(s, 2 * (k + 1)) for k, s in enumerate(sends)]

    g2, u2 = vmem_call(
        combine_kernel, (shape((batch, states), F32), shape((batch, states), BF16)), "combine"
    )(*step(u1), emit, logit, inv)
    main, sums = vmem_call(
        last_kernel, (shape((3, batch, states), F32), shape((batch, 128), F32)), "last"
    )(*step(u2), emit, prior, logit, f1, g2, chain, part, length_col)
    apart = 1
    while apart < cols:
        sums = sums + across(sums, apart)
        apart *= 2
    scaled, like = vmem_call(
        finish_kernel, (shape((batch, states), F32), shape((batch, 128), F32)), "finish"
    )(main, sums, part, length_col)
    return scaled, like[:, 0]


def solution(mesh):
    in_specs = (P("col", None), P(), P(), P(), P(), P(), P("col"), P(), P("grp", None), P("grp"))
    out_specs = (P("grp", "col"), P("grp"))
    return jax.shard_map(
        per_device, mesh=mesh, in_specs=in_specs, out_specs=out_specs, check_vma=False
    )
```

```python
import math

import jax
import jax.numpy as jnp
from jax import lax
from jax.experimental import pallas as pl
from jax.experimental.pallas import tpu as pltpu
from jax.sharding import PartitionSpec as P

SOFT_CAP = 10.0
EMIT_SCALE = 2.0**20
F32 = jnp.float32
BF16 = jnp.bfloat16
NT = (((1,), (1,)), ((), ()))
NN = (((1,), (0,)), ((), ()))


def dot(lhs, rhs, dims):
    return lax.dot_general(lhs, rhs, dims, preferred_element_type=F32)


def across(shard, apart, axis="col"):
    return lax.ppermute(shard, axis, [(i, i ^ apart) for i in range(lax.axis_size(axis))])


def call(body, out_shape, name, smem=(), hbm=(), scratch=(), limit=16, aliases=None):
    def run(*args):
        def space(k):
            if k in smem:
                return pltpu.SMEM
            return pltpu.HBM if k in hbm else pltpu.VMEM

        return pl.pallas_call(
            body,
            out_shape=out_shape,
            in_specs=[pl.BlockSpec(memory_space=space(k)) for k in range(len(args))],
            out_specs=jax.tree.map(lambda s: pl.BlockSpec(memory_space=pltpu.VMEM), out_shape),
            scratch_shapes=scratch,
            input_output_aliases=aliases or {},
            name=name,
            compiler_params=pltpu.CompilerParams(vmem_limit_bytes=limit << 20),
        )(
            *(
                pltpu.with_memory_space_constraint(arg, pltpu.HBM) if k in hbm else arg
                for k, arg in enumerate(args)
            )
        )

    return run


def shape(dims, dtype):
    return jax.ShapeDtypeStruct(dims, dtype)


def capped_exp(values, scale):
    return jnp.exp2((SOFT_CAP / math.log(2.0)) * jnp.tanh(values * (scale / SOFT_CAP)))


def project_kernel(emb_hbm, weight_hbm, out, emb, weight, sem):
    copies = [
        pltpu.make_async_copy(emb_hbm, emb, sem.at[0]),
        pltpu.make_async_copy(weight_hbm, weight, sem.at[1]),
    ]
    for copy in copies:
        copy.start()
    for copy in copies:
        copy.wait()
    out[...] = dot(emb[...], weight[...], NN).astype(BF16)


def emission_kernel(
    tile,
    emb_hbm,
    from_hbm,
    emit_hbm,
    code_hbm,
    init_vec,
    codes,
    from_out,
    prior_out,
    pick_out,
    total_out,
    emb,
    from_w,
    emit_w,
    code,
    sem,
    code_sem,
):
    vocab = code.shape[0]
    tiles = vocab // tile
    own_tiles = tiles // lax.axis_size("grp")
    first = lax.axis_index("grp") * own_tiles
    copies = [
        pltpu.make_async_copy(src, dst, sem.at[k])
        for k, (src, dst) in enumerate(
            ((emb_hbm, emb), (emit_hbm, emit_w), (from_hbm, from_w))
        )
    ]
    starts = []
    for k in range(tiles):
        start = lax.rem(first + k, tiles) * tile
        start = pl.multiple_of(start, tile)
        starts.append(start)
        copies.append(
            pltpu.make_async_copy(
                code_hbm.at[pl.ds(start, tile)], code.at[pl.ds(k * tile, tile)], code_sem.at[k]
            )
        )
    for copy in copies:
        copy.start()
    copies[0].wait()
    copies[1].wait()
    query = dot(emb[...], emit_w[...], NN).astype(BF16)
    states = emb.shape[0]
    prior = dot(jnp.broadcast_to(init_vec[...].reshape(1, -1), (8, emb.shape[1])), emb[...], NT)
    prior_out[...] = capped_exp(prior, 2.0)[:1]
    copies[2].wait()
    from_out[...] = dot(emb[...], from_w[...], NN).astype(BF16)
    steps, batch = codes.shape
    ids = jnp.concatenate([column(codes[t : t + 1, :]) for t in range(steps)], axis=0)
    rows = jnp.zeros((batch * steps, code.shape[1]), F32)
    total = jnp.zeros((8, states), F32)
    for k in range(tiles):
        copies[3 + k].wait()
        block = code[k * tile : (k + 1) * tile, :]
        lanes = lax.broadcasted_iota(jnp.int32, (batch * steps, tile), 1) + starts[k]
        lanes = lanes.astype(F32)
        one_hot = jnp.where(lanes == ids, 1.0, 0.0).astype(BF16)
        rows = rows + dot(one_hot, block, NN)
        if k < own_tiles:
            weights = capped_exp(dot(block, query, NT), 3.0)
            total = total + jnp.sum(weights.reshape(tile // 8, 8, states), axis=0)
    total_out[...] = jnp.sum(total, axis=0, keepdims=True)
    pick_out[...] = capped_exp(dot(rows.astype(BF16), query, NT), 3.0)


def column(row):
    count = row.shape[1]
    at_row = lax.broadcasted_iota(jnp.int32, (count, count), 0)
    at_lane = lax.broadcasted_iota(jnp.int32, (count, count), 1)
    return row_sum(jnp.where(at_row == at_lane, row.astype(F32), 0.0))


def lane_pack(columns, rows):
    lane = lax.broadcasted_iota(jnp.int32, (rows, 128), 1)
    packed = jnp.zeros((rows, 128), F32)
    for k, column in enumerate(columns):
        packed = jnp.where(lane == k, column, packed)
    return packed


def lane_pick(packed, k):
    lane = lax.broadcasted_iota(jnp.int32, packed.shape, 1)
    return jnp.sum(jnp.where(lane == k, packed, 0.0), axis=1, keepdims=True)


def split(packed):
    high = packed.astype(BF16).astype(F32)
    return (high + pltpu.roll(packed - high, 64, 1)).astype(BF16)


def joined(pair):
    pair = pair.astype(F32)
    return pair + pltpu.roll(pair, 64, 1)


def row_sum(values):
    return jnp.sum(values, axis=1, keepdims=True)


def hidden_kernel(pick, total_a, total_b, prior, logit, emit_out, msg_out, mass_out):
    batch = pick.shape[0] // 4
    factor = EMIT_SCALE / (total_a[...] + total_b[...])
    emit = pick[...] * factor
    emit_out[...] = emit
    p = prior[...]
    restart = jax.nn.sigmoid(logit[...])
    first = p * emit[:batch]
    third = p * emit[2 * batch : 3 * batch]
    states = p.shape[1]
    msg_out[:batch, :states] = first * (1.0 - restart)
    msg_out[batch:, :states] = third * (1.0 - restart)
    mass = row_sum(first * restart)
    norm = jnp.broadcast_to(row_sum(p), mass.shape)
    packed = lane_pack([mass, norm], batch)
    msg_out[:batch, states:] = packed
    msg_out[batch:, states:] = jnp.zeros((batch, 128), F32)
    mass_out[...] = packed


def weights_kernel(scale, shifts, mask, from_a, from_b, *refs):
    states = from_a.shape[0]
    count = len(shifts)
    blocks, outs = refs[:count], refs[len(refs) - count - 1 : -1]
    before, sum_out = refs[count : len(refs) - count - 1], refs[-1]
    place = lax.rem(lax.axis_index("col"), mask.shape[0])
    tile = states // 2
    for side, source in ((0, from_a), (1, from_b)):
        lanes = slice(side * states, (side + 1) * states)
        sums = jnp.zeros((8, states), F32)
        for shift, block, out in zip(shifts, blocks, outs):
            row = lax.axis_index("col") ^ shift
            keep = mask[place ^ side, row].astype(F32)
            for k in range(2):
                rows = slice(k * tile, (k + 1) * tile)
                weights = capped_exp(dot(block[rows, :], source[...], NT), scale) * keep
                out[rows, lanes] = weights.astype(BF16)
                sums = sums + jnp.sum(weights.reshape(tile // 8, 8, states), axis=0)
        summed = jnp.sum(sums, axis=0, keepdims=True)
        for other in before:
            summed = summed + other[:, lanes]
        sum_out[:, lanes] = summed


def first_kernel(
    msg_a, msg_b, sums_own, sums_sib, mass, emit, w0, w1, w2, w3, own, s1, s2, s3, inv_out
):
    states = w0.shape[0]
    batch = mass.shape[0]
    inv_a = 1.0 / (sums_own[:, :states] + sums_sib[:, states:])
    inv_b = 1.0 / (sums_own[:, states:] + sums_sib[:, :states])
    inv_out[...] = inv_a
    u_a = (msg_a[:, :states] * inv_a).astype(BF16)
    u_b = (msg_b[:, :states] * inv_b).astype(BF16)
    u = jnp.concatenate([u_a, u_b], axis=1)
    own[...] = dot(u, w0[...], NT)
    pair = split(mass[...])
    last = emit[3 * batch :].astype(BF16)
    for w, s in ((w1, s1), (w2, s2), (w3, s3)):
        s[: 2 * batch, :states] = dot(u, w[...], NT).astype(BF16)
        s[2 * batch :, :states] = last
        s[:batch, states:] = pair
        s[batch:, states:] = jnp.zeros((2 * batch, 128), BF16)


def combine_first_kernel(
    own, r1, r2, r3, mass, emit, prior, logit, inv, f_out, chain_out, u_out, part_out
):
    states = own.shape[1]
    batch = mass.shape[0]
    summed = own[...]
    total = mass[...]
    for r in (r1, r2, r3):
        summed = summed + r[: 2 * batch, :states].astype(F32)
        total = total + joined(r[:batch, states:])
    norm = lane_pick(total, 1)
    ratio = lane_pick(total, 0) / norm
    p = prior[...]
    restart = jax.nn.sigmoid(logit[...])
    f = emit[batch : 2 * batch] * (summed[:batch] + p * ratio)
    f_out[...] = f
    chain_out[...] = emit[3 * batch :] * summed[batch:]
    u_out[...] = (f * (1.0 - restart) * inv[...]).astype(BF16)
    part_out[...] = lane_pack([norm, row_sum(f * restart)], batch)


def backward_kernel(emit, r1, r2, r3, w0, w1, w2, w3, out):
    states = w0.shape[0]
    batch = out.shape[0]
    acc = dot(emit[3 * batch :].astype(BF16), w0[...], NN)
    for r, w in ((r1, w1), (r2, w2), (r3, w3)):
        acc = acc + dot(r[2 * batch :, :states], w[...], NN)
    out[...] = acc


def step_kernel(u_a, u_b, w0, w1, w2, w3, own, s1, s2, s3):
    states = w0.shape[0]
    u_a = u_a[:, :states]
    u_b = u_b[:, :states]
    u = jnp.concatenate([u_a, u_b], axis=1)
    own[...] = dot(u, w0[...], NT)
    for w, s in ((w1, s1), (w2, s2), (w3, s3)):
        s[:, :states] = dot(u, w[...], NT).astype(BF16)


def combine_kernel(
    own, r1, r2, r3, emit, prior, logit, inv, f1, chain, part, lengths, g_out, msg_out
):
    batch, states = own.shape
    summed = own[...]
    for r in (r1, r2, r3):
        summed = summed + r[...].astype(F32)
    restart = jax.nn.sigmoid(logit[...])
    p = prior[...]
    e = emit[...]
    length = column(lengths[...])
    g = e[2 * batch : 3 * batch] * summed
    g_out[...] = g
    msg_out[:, :states] = (g * (1.0 - restart) * inv[...]).astype(BF16)
    h2 = p * e[2 * batch : 3 * batch]
    main = jnp.where(length == 1, p * e[:batch], jnp.where(length == 2, f1[...], g))
    side = jnp.where(length == 3, h2, chain[...])
    packed = lane_pack(
        [
            lane_pick(part[...], 1),
            row_sum(g * restart),
            row_sum(h2 * restart),
            jnp.where(length < 4, row_sum(main), 0.0),
            jnp.where(length >= 3, row_sum(side), 0.0),
            jnp.where(length >= 4, row_sum(p * e[3 * batch :]), 0.0),
        ],
        batch,
    )
    msg_out[:, states:] = split(packed)


def totals_kernel(msg_a, msg_b, back_a, back_b, lengths, out):
    states = msg_a.shape[1] - 128
    u_a = msg_a[:, :states].astype(F32)
    u_b = msg_b[:, :states].astype(F32)
    total = joined(msg_a[:, states:]) + joined(msg_b[:, states:])
    last = u_a * (back_a[:, :states] + back_b[:, states:])
    last = row_sum(last + u_b * (back_a[:, states:] + back_b[:, :states]))
    lane = lax.broadcasted_iota(jnp.int32, total.shape, 1)
    total = jnp.where(lane < 6, total, 0.0)
    out[...] = total + jnp.where((lane == 3) & (column(lengths[...]) == 4), last, 0.0)


def attach_kernel(total, s1, s2, s3, o1, o2, o3):
    states = s1.shape[1] - 128
    pair = split(total[...])
    for out in (o1, o2, o3):
        out[:, states:] = pair


def finish_kernel(
    own, r1, r2, r3, totals, emit, prior, f1, g2, chain, part, lengths, scaled_out, like_out
):
    batch, states = own.shape
    summed = own[...]
    total = totals[...]
    for r in (r1, r2, r3):
        summed = summed + r[:, :states].astype(F32)
        total = total + joined(r[:, states:])
    p = prior[...]
    e = emit[...]
    length = column(lengths[...])
    z = lane_pick(part[...], 0)
    mass1 = lane_pick(total, 0) / z
    mass2 = (lane_pick(total, 1) + mass1 * lane_pick(total, 2)) / z
    full = lane_pick(total, 3) + mass1 * lane_pick(total, 4) + mass2 * lane_pick(total, 5)
    f2 = g2[...] + mass1 * (p * e[2 * batch : 3 * batch])
    f3 = e[3 * batch :] * (summed + p * mass2) + mass1 * chain[...]
    values = jnp.where(
        length == 1,
        p * e[:batch],
        jnp.where(length == 2, f1[...], jnp.where(length == 3, f2, f3)),
    )
    scaled_out[...] = values / full
    like = jnp.log(full) - jnp.log(z) - length * math.log(EMIT_SCALE)
    diagonal = lax.broadcasted_iota(jnp.int32, (batch, batch), 0) == lax.broadcasted_iota(
        jnp.int32, (batch, batch), 1
    )
    like_out[...] = jnp.sum(jnp.where(diagonal, like, 0.0), axis=0, keepdims=True)


def per_device(
    state_emb,
    from_weight,
    to_weight,
    emit_weight,
    code_emb,
    init_vec,
    restart_logit,
    block_mask,
    codes,
    lengths,
):
    states, width = state_emb.shape
    vocab = code_emb.shape[0]
    cluster = block_mask.shape[1]
    batch, steps = codes.shape
    cols = lax.axis_size("col")
    logit = restart_logit.reshape(1, states)
    length_row = lengths.reshape(1, batch)
    square = shape((states, width), BF16)
    plane = shape((batch, states), F32)
    lanes = shape((batch, 128), F32)
    half_plane = shape((batch, states), BF16)
    message = shape((batch, states + 128), BF16)

    to_own = call(
        project_kernel,
        square,
        "to_part",
        hbm=(0, 1),
        scratch=[
            pltpu.VMEM((states, width), BF16),
            pltpu.VMEM((width, width), BF16),
            pltpu.SemaphoreType.DMA((2,)),
        ],
        limit=32,
    )(state_emb, to_weight)
    to_y = across(to_own, 2)
    to_z = across(to_own, 4)

    tile = 512
    from_own, prior, pick, total = call(
        lambda *refs: emission_kernel(tile, *refs),
        (
            square,
            shape((1, states), F32),
            shape((batch * steps, states), F32),
            shape((1, states), F32),
        ),
        "emission",
        hbm=(0, 1, 2, 3),
        scratch=[
            pltpu.VMEM((states, width), BF16),
            pltpu.VMEM((width, width), BF16),
            pltpu.VMEM((width, width), BF16),
            pltpu.VMEM((vocab, width), BF16),
            pltpu.SemaphoreType.DMA((3,)),
            pltpu.SemaphoreType.DMA((vocab // tile,)),
        ],
        limit=32,
    )(state_emb, from_weight, emit_weight, code_emb, init_vec, codes.T)
    from_sib = across(from_own, 1)
    total_other = across(total, 1, "grp")

    half = states // 2
    to_d0 = across(to_z[:half], 2)
    to_d1 = across(to_y[half:], 4)

    emit, msg, mass_own = call(
        hidden_kernel,
        (shape((batch * steps, states), F32), shape((2 * batch, states + 128), F32), lanes),
        "hidden",
    )(pick, total, total_other, prior, logit)
    msg_sib = across(msg, 1)

    scale = 2.0 / math.sqrt(width)
    sums_shape = shape((1, 2 * states), F32)
    wt_shape = shape((states, 2 * states), BF16)
    w0, sums0 = call(
        lambda *refs: weights_kernel(scale, (0,), *refs), (wt_shape, sums_shape), "weights", (0,)
    )(block_mask.T, from_own, from_sib, to_own)
    w1, w2, sums1 = call(
        lambda *refs: weights_kernel(scale, (2, 4), *refs),
        (wt_shape, wt_shape, sums_shape),
        "weights",
        (0,),
    )(block_mask.T, from_own, from_sib, to_y, to_z, sums0)
    mass = mass_own + msg_sib[:batch, states:]
    apart = cluster
    while apart < cols:
        mass = mass + across(mass, apart)
        apart *= 2
    to_d = jnp.concatenate([to_d0, to_d1], axis=0)
    w3, row_sums = call(
        lambda *refs: weights_kernel(scale, (6,), *refs), (wt_shape, sums_shape), "weights", (0,)
    )(block_mask.T, from_own, from_sib, to_d, sums1)
    wts = (w0, w1, w2, w3)
    row_sums_sib = across(row_sums, 1)

    out = call(
        first_kernel,
        (shape((2 * batch, states), F32),)
        + (shape((3 * batch, states + 128), BF16),) * 3
        + (shape((1, states), F32),),
        "first",
    )(msg, msg_sib, row_sums, row_sums_sib, mass, emit, *wts)
    own, sends, inv = out[0], out[1:4], out[4]
    received = [across(s, 2 * (k + 1)) for k, s in enumerate(sends)]
    f1, chain, u1, part = call(
        combine_first_kernel, (plane, plane, half_plane, lanes), "combine_first"
    )(own, *received, mass, emit, prior, logit, inv)
    u1_sib = across(u1, 1)
    held, _ = lax.optimization_barrier((tuple(received), u1))
    back = call(backward_kernel, shape((batch, 2 * states), F32), "backward")(emit, *held, *wts)
    own, *sends = call(step_kernel, (plane,) + (half_plane,) * 3, "step")(u1, u1_sib, *wts)
    back_sib = across(back, 1)
    received = [across(s, 2 * (k + 1)) for k, s in enumerate(sends)]
    g2, msg2 = call(combine_kernel, (plane, message), "combine")(
        own, *received, emit, prior, logit, inv, f1, chain, part, length_row
    )
    msg2_sib = across(msg2, 1)
    totals = call(totals_kernel, lanes, "totals")(msg2, msg2_sib, back, back_sib, length_row)
    own, *sends = call(step_kernel, (plane,) + (message,) * 3, "step")(msg2, msg2_sib, *wts)
    apart = cluster
    while apart < cols:
        totals = totals + across(totals, apart)
        apart *= 2
    sends = call(attach_kernel, (message,) * 3, "attach", aliases={1: 0, 2: 1, 3: 2})(
        totals, *sends
    )
    received = [across(s, 2 * (k + 1)) for k, s in enumerate(sends)]
    scaled, like = call(finish_kernel, (plane, shape((1, batch), F32)), "finish")(
        own, *received, totals, emit, prior, f1, g2, chain, part, length_row
    )
    return scaled, like.reshape(batch)


def solution(mesh):
    in_specs = (P("col", None), P(), P(), P(), P(), P(), P("col"), P(), P("grp", None), P("grp"))
    out_specs = (P("grp", "col"), P("grp"))
    return jax.shard_map(
        per_device, mesh=mesh, in_specs=in_specs, out_specs=out_specs, check_vma=False
    )
```

```python
import math

import jax
import jax.numpy as jnp
from jax import lax
from jax.experimental import pallas as pl
from jax.experimental.pallas import tpu as pltpu
from jax.sharding import PartitionSpec as P

SOFT_CAP = 10.0
EMIT_SCALE = 2.0**20
F32 = jnp.float32
BF16 = jnp.bfloat16
NT = (((1,), (1,)), ((), ()))
NN = (((1,), (0,)), ((), ()))


def dot(lhs, rhs, dims):
    return lax.dot_general(lhs, rhs, dims, preferred_element_type=F32)


def across(shard, apart, axis="col"):
    return lax.ppermute(shard, axis, [(i, i ^ apart) for i in range(lax.axis_size(axis))])


def call(body, out_shape, name, smem=(), hbm=(), scratch=(), limit=32, aliases=None, micros=0.2):
    def run(*args):
        def space(k):
            if k in smem:
                return pltpu.SMEM
            return pltpu.HBM if k in hbm else pltpu.VMEM

        return pl.pallas_call(
            body,
            out_shape=out_shape,
            in_specs=[pl.BlockSpec(memory_space=space(k)) for k in range(len(args))],
            out_specs=jax.tree.map(lambda s: pl.BlockSpec(memory_space=pltpu.VMEM), out_shape),
            scratch_shapes=scratch,
            input_output_aliases=aliases or {},
            name=name,
            cost_estimate=pl.CostEstimate(
                flops=int(micros * 1e9), bytes_accessed=int(micros * 3e6), transcendentals=0
            ),
            compiler_params=pltpu.CompilerParams(vmem_limit_bytes=limit << 20),
        )(
            *(
                pltpu.with_memory_space_constraint(arg, pltpu.HBM) if k in hbm else arg
                for k, arg in enumerate(args)
            )
        )

    return run


def shape(dims, dtype):
    return jax.ShapeDtypeStruct(dims, dtype)


def capped_exp(values, scale):
    return jnp.exp2((SOFT_CAP / math.log(2.0)) * jnp.tanh(values * (scale / SOFT_CAP)))


def project_kernel(
    emb_hbm, weight_hbm, emit_hbm, from_hbm, top, bottom, emb, emit_w, from_out, weight, from_w, sem
):
    pairs = ((emb_hbm, emb), (weight_hbm, weight), (emit_hbm, emit_w), (from_hbm, from_w))
    copies = [pltpu.make_async_copy(src, dst, sem.at[k]) for k, (src, dst) in enumerate(pairs)]
    for copy in copies:
        copy.start()
    copies[0].wait()
    copies[1].wait()
    half = top.shape[0]
    bottom[...] = dot(emb[half:, :], weight[...], NN).astype(BF16)
    top[...] = dot(emb[:half, :], weight[...], NN).astype(BF16)
    copies[3].wait()
    from_out[...] = dot(emb[...], from_w[...], NN).astype(BF16)
    copies[2].wait()


def emission_kernel(
    tile,
    emb,
    emit_w,
    code,
    logit,
    init_hbm,
    ids_hbm,
    prior_out,
    emit_out,
    msg_out,
    mass_out,
    one_hot,
    init_vec,
    codes,
    sem,
):
    copies = [
        pltpu.make_async_copy(init_hbm, init_vec, sem.at[0]),
        pltpu.make_async_copy(ids_hbm, codes, sem.at[1]),
    ]
    for copy in copies:
        copy.start()
    query = dot(emb[...], emit_w[...], NN).astype(BF16)
    states = emb.shape[0]
    tiles = code.shape[0] // tile
    total = jnp.zeros((8, states), F32)
    for k in range(tiles):
        weights = capped_exp(dot(code[k * tile : (k + 1) * tile, :], query, NT), 3.0)
        total = total + jnp.sum(weights.reshape(tile // 8, 8, states), axis=0)
    for copy in copies:
        copy.wait()
    prior = dot(jnp.broadcast_to(init_vec[...].reshape(1, -1), (8, emb.shape[1])), emb[...], NT)
    p = capped_exp(prior, 2.0)[:1]
    prior_out[...] = p
    steps, batch = codes.shape
    ids = jnp.concatenate([column(codes[t : t + 1, :]) for t in range(steps)], axis=0)
    lanes = lax.broadcasted_iota(jnp.int32, (batch * steps, tile), 1).astype(F32)
    for k in range(tiles):
        hit = lanes == ids - float(k * tile)
        one_hot[:, k * tile : (k + 1) * tile] = jnp.where(hit, 1.0, 0.0).astype(BF16)
    rows = dot(one_hot[...], code[...], NN)
    factor = EMIT_SCALE / jnp.sum(total, axis=0, keepdims=True)
    emit = capped_exp(dot(rows.astype(BF16), query, NT), 3.0) * factor
    emit_out[...] = emit
    restart = jax.nn.sigmoid(logit[...])
    first = p * emit[:batch]
    third = p * emit[2 * batch : 3 * batch]
    msg_out[:batch, :states] = first * (1.0 - restart)
    msg_out[batch:, :states] = third * (1.0 - restart)
    mass = row_sum(first * restart)
    packed = lane_pack([mass, jnp.broadcast_to(row_sum(p), mass.shape)], batch)
    msg_out[:batch, states:] = packed
    msg_out[batch:, states:] = jnp.zeros((batch, 128), F32)
    mass_out[...] = packed


def column(row):
    count = row.shape[1]
    at_row = lax.broadcasted_iota(jnp.int32, (count, count), 0)
    at_lane = lax.broadcasted_iota(jnp.int32, (count, count), 1)
    return row_sum(jnp.where(at_row == at_lane, row.astype(F32), 0.0))


def lane_pack(columns, rows):
    lane = lax.broadcasted_iota(jnp.int32, (rows, 128), 1)
    packed = jnp.zeros((rows, 128), F32)
    for k, column in enumerate(columns):
        packed = jnp.where(lane == k, column, packed)
    return packed


def lane_pick(packed, k):
    lane = lax.broadcasted_iota(jnp.int32, packed.shape, 1)
    return jnp.sum(jnp.where(lane == k, packed, 0.0), axis=1, keepdims=True)


def split(packed):
    high = packed.astype(BF16).astype(F32)
    rest = packed - high
    middle = rest.astype(BF16).astype(F32)
    return (high + pltpu.roll(middle, 32, 1) + pltpu.roll(rest - middle, 64, 1)).astype(BF16)


def joined(parts):
    parts = parts.astype(F32)
    return parts + pltpu.roll(parts, 96, 1) + pltpu.roll(parts, 64, 1)


def row_sum(values):
    return jnp.sum(values, axis=1, keepdims=True)


def weights_kernel(scale, shifts, mask, from_a, from_b, *refs):
    states = from_a.shape[0]
    count = len(shifts)
    blocks, outs = refs[: 2 * count], refs[len(refs) - count - 1 : -1]
    before, sum_out = refs[2 * count : len(refs) - count - 1], refs[-1]
    place = lax.rem(lax.axis_index("col"), mask.shape[0])
    tile = states // 2
    for side, source in ((0, from_a), (1, from_b)):
        rows = slice(side * states, (side + 1) * states)
        sums = before[0][rows, :] if before else jnp.zeros((states, 128), F32)
        for n, (shift, out) in enumerate(zip(shifts, outs)):
            row = lax.axis_index("col") ^ shift
            keep = mask[place ^ side, row].astype(F32)
            for k in range(2):
                block = blocks[2 * n + k]
                weights = capped_exp(dot(source[...], block[...], NT), scale) * keep
                out[rows, k * tile : (k + 1) * tile] = weights.astype(BF16)
                for lane in range(0, tile, 128):
                    sums = sums + weights[:, lane : lane + 128]
        if sum_out.shape[0] == 1:
            sum_out[:, rows] = jnp.sum(sums.T, axis=0, keepdims=True)
        else:
            sum_out[rows, :] = sums


def first_kernel(
    msg_a, msg_b, sums_own, sums_sib, mass, emit, w0, w1, w2, w3, own, s1, s2, s3, inv_out, u_out
):
    states = w0.shape[1]
    batch = mass.shape[0]
    inv_a = 1.0 / (sums_own[:, :states] + sums_sib[:, states:])
    inv_b = 1.0 / (sums_own[:, states:] + sums_sib[:, :states])
    inv_out[...] = inv_a
    u_a = (msg_a[:, :states] * inv_a).astype(BF16)
    u_b = (msg_b[:, :states] * inv_b).astype(BF16)
    u = jnp.concatenate([u_a, u_b], axis=1)
    u_out[...] = u[batch:]
    u = u[:batch]
    own[...] = dot(u, w0[...], NN)
    parts = split(mass[...])
    last = emit[3 * batch :].astype(BF16)
    for w, s in ((w1, s1), (w2, s2), (w3, s3)):
        s[:batch, :states] = dot(u, w[...], NN).astype(BF16)
        s[batch:, :states] = last
        s[:batch, states:] = parts
        s[batch:, states:] = jnp.zeros((batch, 128), BF16)


def combine_first_kernel(own, r1, r2, r3, mass, emit, prior, logit, inv, f_out, u_out, part_out):
    batch, states = own.shape
    summed = own[...]
    total = mass[...]
    for r in (r1, r2, r3):
        summed = summed + r[:batch, :states].astype(F32)
        total = total + joined(r[:batch, states:])
    norm = lane_pick(total, 1)
    ratio = lane_pick(total, 0) / norm
    restart = jax.nn.sigmoid(logit[...])
    f = emit[batch : 2 * batch] * (summed + prior[...] * ratio)
    f_out[...] = f
    u_out[...] = (f * (1.0 - restart) * inv[...]).astype(BF16)
    part_out[...] = lane_pack([norm, row_sum(f * restart)], batch)


def backward_kernel(emit, r1, r2, r3, w0, w1, w2, w3, out):
    states = w0.shape[1]
    batch = out.shape[0]
    acc = dot(emit[3 * batch :].astype(BF16), w0[...], NT)
    for r, w in ((r1, w1), (r2, w2), (r3, w3)):
        acc = acc + dot(r[batch:, :states], w[...], NT)
    out[...] = acc


def second_kernel(u_a, u_b, u_chain, w0, w1, w2, w3, own, s1, s2, s3):
    u = jnp.concatenate([jnp.concatenate([u_a[...], u_b[...]], axis=1), u_chain[...]], axis=0)
    own[...] = dot(u, w0[...], NN)
    for w, s in ((w1, s1), (w2, s2), (w3, s3)):
        s[...] = dot(u, w[...], NN).astype(BF16)


def third_kernel(u_a, u_b, w0, w1, w2, w3, own, s1, s2, s3):
    states = w0.shape[1]
    u = jnp.concatenate([u_a[:, :states], u_b[:, :states]], axis=1)
    own[...] = dot(u, w0[...], NN)
    for w, s in ((w1, s1), (w2, s2), (w3, s3)):
        s[:, :states] = dot(u, w[...], NN).astype(BF16)


def combine_kernel(
    own,
    r1,
    r2,
    r3,
    emit,
    prior,
    logit,
    inv,
    f1,
    part,
    back_a,
    back_b,
    lengths,
    g_out,
    chain_out,
    msg_out,
    pack_out,
):
    batch, states = f1.shape
    summed = own[...]
    for r in (r1, r2, r3):
        summed = summed + r[...].astype(F32)
    restart = jax.nn.sigmoid(logit[...])
    p = prior[...]
    e = emit[...]
    length = column(lengths[...])
    g = e[2 * batch : 3 * batch] * summed[:batch]
    g_out[...] = g
    chain = e[3 * batch :] * summed[batch:]
    chain_out[...] = chain
    u = (g * (1.0 - restart) * inv[...]).astype(BF16)
    msg_out[:, :states] = u
    last = row_sum(u.astype(F32) * (back_a[:, :states] + back_b[:, states:]))
    h2 = p * e[2 * batch : 3 * batch]
    main = jnp.where(length == 1, p * e[:batch], jnp.where(length == 2, f1[...], g))
    side = jnp.where(length == 3, h2, chain)
    packed = lane_pack(
        [
            lane_pick(part[...], 1),
            row_sum(g * restart),
            row_sum(h2 * restart),
            jnp.where(length < 4, row_sum(main), last),
            jnp.where(length >= 3, row_sum(side), 0.0),
            jnp.where(length >= 4, row_sum(p * e[3 * batch :]), 0.0),
        ],
        batch,
    )
    msg_out[:, states:] = split(packed)
    pack_out[...] = packed


def clean(packed):
    lane = lax.broadcasted_iota(jnp.int32, packed.shape, 1)
    return jnp.where(lane < 6, packed, 0.0)


def totals_kernel(msg_sib, pack, other_a, other_b, out):
    states = msg_sib.shape[1] - 128
    here = pack[...] + joined(msg_sib[:, states:])
    out[...] = clean(here + (other_a[...] + other_b[...]))


def attach_kernel(total, s1, s2, s3, o1, o2, o3):
    states = s1.shape[1] - 128
    parts = split(total[...])
    for out in (o1, o2, o3):
        out[:, states:] = parts


def attach_sum_kernel(msg_sib, pack, other_a, other_b, s1, s2, s3, total, o1, o2, o3):
    totals_kernel(msg_sib, pack, other_a, other_b, total)
    attach_kernel(total, s1, s2, s3, o1, o2, o3)


def finish_kernel(
    own, r1, r2, r3, totals, emit, prior, f1, g2, chain, part, lengths, scaled_out, like_out
):
    batch, states = own.shape
    summed = own[...]
    total = totals[...]
    for r in (r1, r2, r3):
        summed = summed + r[:, :states].astype(F32)
        total = total + joined(r[:, states:])
    p = prior[...]
    e = emit[...]
    length = column(lengths[...])
    z = lane_pick(part[...], 0)
    mass1 = lane_pick(total, 0) / z
    mass2 = (lane_pick(total, 1) + mass1 * lane_pick(total, 2)) / z
    full = lane_pick(total, 3) + mass1 * lane_pick(total, 4) + mass2 * lane_pick(total, 5)
    f2 = g2[...] + mass1 * (p * e[2 * batch : 3 * batch])
    f3 = e[3 * batch :] * (summed + p * mass2) + mass1 * chain[...]
    values = jnp.where(
        length == 1,
        p * e[:batch],
        jnp.where(length == 2, f1[...], jnp.where(length == 3, f2, f3)),
    )
    scaled_out[...] = values / full
    like = jnp.log(full) - jnp.log(z) - length * math.log(EMIT_SCALE)
    diagonal = lax.broadcasted_iota(jnp.int32, (batch, batch), 0) == lax.broadcasted_iota(
        jnp.int32, (batch, batch), 1
    )
    like_out[...] = jnp.sum(jnp.where(diagonal, like, 0.0), axis=0, keepdims=True)


def per_device(
    state_emb,
    from_weight,
    to_weight,
    emit_weight,
    code_emb,
    init_vec,
    restart_logit,
    block_mask,
    codes,
    lengths,
):
    states, width = state_emb.shape
    vocab = code_emb.shape[0]
    cluster = block_mask.shape[1]
    batch, steps = codes.shape
    cols = lax.axis_size("col")
    logit = restart_logit.reshape(1, states)
    length_row = lengths.reshape(1, batch)
    square = shape((states, width), BF16)
    plane = shape((batch, states), F32)
    lanes = shape((batch, 128), F32)
    half_plane = shape((batch, states), BF16)
    message = shape((batch, states + 128), BF16)

    half = states // 2
    half_block = shape((half, width), BF16)
    top, bottom, emb, emit_w, from_own = call(
        project_kernel,
        (half_block, half_block) + (square,) * 3,
        "to_part",
        hbm=(0, 1, 2, 3),
        micros=6,
        scratch=[
            pltpu.VMEM((width, width), BF16),
            pltpu.VMEM((width, width), BF16),
            pltpu.SemaphoreType.DMA((4,)),
        ],
    )(state_emb, to_weight, emit_weight, from_weight)
    y_bottom = across(bottom, 2)
    z_top = across(top, 4)
    y_top = across(top, 2)
    z_bottom = across(bottom, 4)

    from_sib = across(from_own, 1)
    prior, emit, msg, mass_own = call(
        lambda *refs: emission_kernel(512, *refs),
        (
            shape((1, states), F32),
            shape((batch * steps, states), F32),
            shape((2 * batch, states + 128), F32),
            lanes,
        ),
        "emission",
        hbm=(4, 5),
        micros=0.5,
        scratch=[
            pltpu.VMEM((batch * steps, vocab), BF16),
            pltpu.VMEM((width,), BF16),
            pltpu.VMEM((steps, batch), jnp.int32),
            pltpu.SemaphoreType.DMA((2,)),
        ],
    )(emb, emit_w, code_emb, logit, init_vec, codes.T)

    scale = 2.0 / math.sqrt(width)
    sums_shape = shape((2 * states, 128), F32)
    wt_shape = shape((2 * states, states), BF16)
    w0, sums0 = call(
        lambda *refs: weights_kernel(scale, (0,), *refs),
        (wt_shape, sums_shape),
        "weights",
        (0,),
        micros=1.5,
    )(block_mask.T, from_own, from_sib, top, bottom)
    d_top = across(z_top, 2)
    d_bottom = across(y_bottom, 4)
    y_top, z_bottom, sums0 = lax.optimization_barrier((y_top, z_bottom, sums0))
    msg, mass_own, *_ = lax.optimization_barrier((msg, mass_own, y_top, z_bottom))
    msg_sib = across(msg, 1)
    w1, w2, sums1 = call(
        lambda *refs: weights_kernel(scale, (2, 4), *refs),
        (wt_shape, wt_shape, sums_shape),
        "weights",
        (0,),
        micros=2,
    )(block_mask.T, from_own, from_sib, y_top, y_bottom, z_top, z_bottom, sums0)
    mass = mass_own + msg_sib[:batch, states:]
    apart = cluster
    while apart < cols:
        mass = mass + across(mass, apart)
        apart *= 2
    w3, row_sums = call(
        lambda *refs: weights_kernel(scale, (6,), *refs),
        (wt_shape, shape((1, 2 * states), F32)),
        "weights",
        (0,),
        micros=1.5,
    )(block_mask.T, from_own, from_sib, d_top, d_bottom, sums1)
    wts = (w0, w1, w2, w3)
    row_sums_sib = across(row_sums, 1)

    out = call(
        first_kernel,
        (plane,)
        + (shape((2 * batch, states + 128), BF16),) * 3
        + (shape((1, states), F32), shape((batch, 2 * states), BF16)),
        "first",
        micros=1,
    )(msg, msg_sib, row_sums, row_sums_sib, mass, emit, *wts)
    own, sends, inv, u_chain = out[0], out[1:4], out[4], out[5]
    received = [across(s, 2 * (k + 1)) for k, s in enumerate(sends)]
    f1, u1, part = call(combine_first_kernel, (plane, half_plane, lanes), "combine_first")(
        own, *received, mass, emit, prior, logit, inv
    )
    u1_sib = across(u1, 1)
    held, _ = lax.optimization_barrier((tuple(received), u1))
    back = call(backward_kernel, shape((batch, 2 * states), F32), "backward", micros=1)(emit, *held, *wts)
    own, *sends = call(
        second_kernel,
        (shape((2 * batch, states), F32),) + (shape((2 * batch, states), BF16),) * 3,
        "second",
        micros=1,
    )(u1, u1_sib, u_chain, *wts)
    back_sib = across(back, 1)
    received = [across(s, 2 * (k + 1)) for k, s in enumerate(sends)]
    g2, chain, msg2, pack = call(combine_kernel, (plane, plane, message, lanes), "combine")(
        own,
        *received,
        emit,
        prior,
        logit,
        inv,
        f1,
        part,
        back,
        back_sib,
        length_row,
    )
    msg2_sib = across(msg2, 1)
    others = [across(pack, cluster), across(pack, cluster + 1)]
    own, *sends = call(third_kernel, (plane,) + (message,) * 3, "third", micros=1)(
        msg2, msg2_sib, *wts
    )
    if cols == 2 * cluster:
        totals, *sends = call(
            attach_sum_kernel, (lanes,) + (message,) * 3, "attach", aliases={4: 1, 5: 2, 6: 3}
        )(msg2_sib, pack, *others, *sends)
    else:
        totals = call(totals_kernel, lanes, "totals")(msg2_sib, pack, *others)
        apart = 2 * cluster
        while apart < cols:
            totals = totals + across(totals, apart)
            apart *= 2
        sends = call(attach_kernel, (message,) * 3, "attach", aliases={1: 0, 2: 1, 3: 2})(
            totals, *sends
        )
    received = [across(s, 2 * (k + 1)) for k, s in enumerate(sends)]
    scaled, like = call(finish_kernel, (plane, shape((1, batch), F32)), "finish")(
        own, *received, totals, emit, prior, f1, g2, chain, part, length_row
    )
    return scaled, like.reshape(batch)


def solution(mesh):
    in_specs = (P("col", None), P(), P(), P(), P(), P(), P("col"), P(), P("grp", None), P("grp"))
    out_specs = (P("grp", "col"), P("grp"))
    return jax.shard_map(
        per_device, mesh=mesh, in_specs=in_specs, out_specs=out_specs, check_vma=False
    )
```

```python
import math

import jax
import jax.numpy as jnp
from jax import lax
from jax.experimental import pallas as pl
from jax.experimental.pallas import tpu as pltpu
from jax.sharding import PartitionSpec as P

SOFT_CAP = 10.0
EMIT_SCALE = 2.0**20
SHIFTS = (6, 2, 4)
F32 = jnp.float32
BF16 = jnp.bfloat16
NT = (((1,), (1,)), ((), ()))
NN = (((1,), (0,)), ((), ()))


def dot(lhs, rhs, dims):
    return lax.dot_general(lhs, rhs, dims, preferred_element_type=F32)


def across(shard, apart, axis="col"):
    return lax.ppermute(shard, axis, [(i, i ^ apart) for i in range(lax.axis_size(axis))])


def call(body, out_shape, name, hbm=(), scratch=(), limit=32, aliases=None, micros=0.2):
    def run(*args):
        def space(k):
            return pltpu.HBM if k in hbm else pltpu.VMEM

        return pl.pallas_call(
            body,
            out_shape=out_shape,
            in_specs=[pl.BlockSpec(memory_space=space(k)) for k in range(len(args))],
            out_specs=jax.tree.map(lambda s: pl.BlockSpec(memory_space=pltpu.VMEM), out_shape),
            scratch_shapes=scratch,
            input_output_aliases=aliases or {},
            name=name,
            cost_estimate=pl.CostEstimate(
                flops=int(micros * 1e9), bytes_accessed=int(micros * 3e6), transcendentals=0
            ),
            compiler_params=pltpu.CompilerParams(vmem_limit_bytes=limit << 20),
        )(
            *(
                pltpu.with_memory_space_constraint(arg, pltpu.HBM) if k in hbm else arg
                for k, arg in enumerate(args)
            )
        )

    return run


def shape(dims, dtype):
    return jax.ShapeDtypeStruct(dims, dtype)


def capped_exp(values, scale):
    return jnp.exp2((SOFT_CAP / math.log(2.0)) * jnp.tanh(values * (scale / SOFT_CAP)))


def halves_kernel(emb_hbm, top, bottom, sem):
    half = top.shape[0]
    copies = [
        pltpu.make_async_copy(emb_hbm.at[pl.ds(half, half)], bottom, sem.at[0]),
        pltpu.make_async_copy(emb_hbm.at[pl.ds(0, half)], top, sem.at[1]),
    ]
    for copy in copies:
        copy.start()
    for copy in copies:
        copy.wait()


def emission_kernel(
    tile,
    top,
    bottom,
    emit_w,
    code,
    logit,
    init_hbm,
    ids_hbm,
    prior_out,
    emit_out,
    msg_out,
    mass_out,
    one_hot,
    init_vec,
    codes,
    sem,
):
    copies = [
        pltpu.make_async_copy(init_hbm, init_vec, sem.at[0]),
        pltpu.make_async_copy(ids_hbm, codes, sem.at[1]),
    ]
    for copy in copies:
        copy.start()
    emb = jnp.concatenate([top[...], bottom[...]], axis=0)
    query = dot(emb, emit_w[...], NN).astype(BF16)
    states = emb.shape[0]
    tiles = code.shape[0] // tile
    total = jnp.zeros((8, states), F32)
    for k in range(tiles):
        weights = capped_exp(dot(code[k * tile : (k + 1) * tile, :], query, NT), 3.0)
        total = total + jnp.sum(weights.reshape(tile // 8, 8, states), axis=0)
    for copy in copies:
        copy.wait()
    prior = dot(jnp.broadcast_to(init_vec[...].reshape(1, -1), (8, emb.shape[1])), emb, NT)
    p = capped_exp(prior, 2.0)[:1]
    prior_out[...] = p
    steps, batch = codes.shape
    ids = jnp.concatenate([column(codes[t : t + 1, :]) for t in range(steps)], axis=0)
    lanes = lax.broadcasted_iota(jnp.int32, (batch * steps, tile), 1).astype(F32)
    for k in range(tiles):
        hit = lanes == ids - float(k * tile)
        one_hot[:, k * tile : (k + 1) * tile] = jnp.where(hit, 1.0, 0.0).astype(BF16)
    rows = dot(one_hot[...], code[...], NN)
    factor = EMIT_SCALE / jnp.sum(total, axis=0, keepdims=True)
    emit = capped_exp(dot(rows.astype(BF16), query, NT), 3.0) * factor
    emit_out[...] = emit
    restart = jax.nn.sigmoid(logit[...])
    first = p * emit[:batch]
    third = p * emit[2 * batch : 3 * batch]
    msg_out[:batch, :states] = first * (1.0 - restart)
    msg_out[batch:, :states] = third * (1.0 - restart)
    mass = row_sum(first * restart)
    packed = lane_pack([mass, jnp.broadcast_to(row_sum(p), mass.shape)], batch)
    msg_out[:batch, states:] = packed
    msg_out[batch:, states:] = jnp.zeros((batch, 128), F32)
    mass_out[...] = packed


def column(row):
    count = row.shape[1]
    at_row = lax.broadcasted_iota(jnp.int32, (count, count), 0)
    at_lane = lax.broadcasted_iota(jnp.int32, (count, count), 1)
    return row_sum(jnp.where(at_row == at_lane, row.astype(F32), 0.0))


def lane_pack(columns, rows):
    lane = lax.broadcasted_iota(jnp.int32, (rows, 128), 1)
    packed = jnp.zeros((rows, 128), F32)
    for k, column in enumerate(columns):
        packed = jnp.where(lane == k, column, packed)
    return packed


def lane_pick(packed, k):
    lane = lax.broadcasted_iota(jnp.int32, packed.shape, 1)
    return jnp.sum(jnp.where(lane == k, packed, 0.0), axis=1, keepdims=True)


def split(packed):
    high = packed.astype(BF16).astype(F32)
    rest = packed - high
    middle = rest.astype(BF16).astype(F32)
    return (high + pltpu.roll(middle, 32, 1) + pltpu.roll(rest - middle, 64, 1)).astype(BF16)


def joined(parts):
    parts = parts.astype(F32)
    return parts + pltpu.roll(parts, 96, 1) + pltpu.roll(parts, 64, 1)


def row_sum(values):
    return jnp.sum(values, axis=1, keepdims=True)


def sources_kernel(scale, mask, to_w, top, bottom, sib, from_w, from_a, from_b, out, sum_out):
    half = top.shape[0]
    from_a[:half, :] = dot(top[...], from_w[...], NN).astype(BF16)
    from_a[half:, :] = dot(bottom[...], from_w[...], NN).astype(BF16)
    from_b[...] = dot(sib[...], from_w[...], NN).astype(BF16)
    weights_kernel(scale, (0,), mask, to_w, from_a, from_b, top, bottom, out, sum_out)


def weights_kernel(scale, shifts, mask, to_w, from_a, from_b, *refs):
    states = from_a.shape[0]
    count = len(shifts)
    blocks, outs = refs[: 2 * count], refs[len(refs) - count - 1 : -1]
    before, sum_out = refs[2 * count : len(refs) - count - 1], refs[-1]
    place = lax.rem(lax.axis_index("col"), mask.shape[0])
    at_place = lax.broadcasted_iota(jnp.int32, mask.shape, 0)
    at_col = lax.broadcasted_iota(jnp.int32, mask.shape, 1)
    tile = states // 2
    targets = [dot(block[...], to_w[...], NN).astype(BF16) for block in blocks]
    for side, source in ((0, from_a), (1, from_b)):
        rows = slice(side * states, (side + 1) * states)
        sums = before[0][rows, :] if before else jnp.zeros((states, 128), F32)
        for n, (shift, out) in enumerate(zip(shifts, outs)):
            row = lax.axis_index("col") ^ shift
            keep = (at_place == place ^ side) & (at_col == row)
            keep = jnp.sum(jnp.where(keep, mask[...], 0).astype(F32), axis=(0, 1), keepdims=True)
            for k in range(2):
                target = targets[2 * n + k]
                weights = capped_exp(dot(source[...], target, NT), scale) * keep
                out[rows, k * tile : (k + 1) * tile] = weights.astype(BF16)
                for lane in range(0, tile, 128):
                    sums = sums + weights[:, lane : lane + 128]
        if sum_out.shape[0] == 1:
            sum_out[:, rows] = jnp.sum(sums.T, axis=0, keepdims=True)
        else:
            sum_out[rows, :] = sums


def first_kernel(
    msg_a, msg_b, sums_own, sums_sib, mass, emit, w0, w1, w2, w3, own, s1, s2, s3, inv_out, u_out
):
    states = w0.shape[1]
    batch = mass.shape[0]
    inv_a = 1.0 / (sums_own[:, :states] + sums_sib[:, states:])
    inv_b = 1.0 / (sums_own[:, states:] + sums_sib[:, :states])
    inv_out[...] = inv_a
    u_a = (msg_a[:, :states] * inv_a).astype(BF16)
    u_b = (msg_b[:, :states] * inv_b).astype(BF16)
    u = jnp.concatenate([u_a, u_b], axis=1)
    u_out[...] = u[batch:]
    u = u[:batch]
    own[...] = dot(u, w0[...], NN)
    parts = split(mass[...])
    last = emit[3 * batch :].astype(BF16)
    for w, s in ((w1, s1), (w2, s2), (w3, s3)):
        s[:batch, :states] = dot(u, w[...], NN).astype(BF16)
        s[batch:, :states] = last
        s[:batch, states:] = parts
        s[batch:, states:] = jnp.zeros((batch, 128), BF16)


def combine_first_kernel(own, r1, r2, r3, mass, emit, prior, logit, inv, f_out, u_out, part_out):
    batch, states = own.shape
    summed = own[...]
    total = mass[...]
    for r in (r1, r2, r3):
        summed = summed + r[:batch, :states].astype(F32)
        total = total + joined(r[:batch, states:])
    norm = lane_pick(total, 1)
    ratio = lane_pick(total, 0) / norm
    restart = jax.nn.sigmoid(logit[...])
    f = emit[batch : 2 * batch] * (summed + prior[...] * ratio)
    f_out[...] = f
    u_out[...] = (f * (1.0 - restart) * inv[...]).astype(BF16)
    part_out[...] = lane_pack([norm, row_sum(f * restart)], batch)


def backward_kernel(emit, r1, r2, r3, w0, w1, w2, w3, out):
    states = w0.shape[1]
    batch = out.shape[0]
    acc = dot(emit[3 * batch :].astype(BF16), w0[...], NT)
    for r, w in ((r1, w1), (r2, w2), (r3, w3)):
        acc = acc + dot(r[batch:, :states], w[...], NT)
    out[...] = acc


def second_kernel(u_a, u_b, u_chain, w0, w1, w2, w3, own, s1, s2, s3):
    u = jnp.concatenate([jnp.concatenate([u_a[...], u_b[...]], axis=1), u_chain[...]], axis=0)
    own[...] = dot(u, w0[...], NN)
    for w, s in ((w1, s1), (w2, s2), (w3, s3)):
        s[...] = dot(u, w[...], NN).astype(BF16)


def third_kernel(u_a, u_b, w0, w1, w2, w3, own, s1, s2, s3):
    states = w0.shape[1]
    u = jnp.concatenate([u_a[:, :states], u_b[:, :states]], axis=1)
    own[...] = dot(u, w0[...], NN)
    for w, s in ((w1, s1), (w2, s2), (w3, s3)):
        s[:, :states] = dot(u, w[...], NN).astype(BF16)


def combine_kernel(
    own,
    r1,
    r2,
    r3,
    emit,
    prior,
    logit,
    inv,
    f1,
    part,
    back_a,
    back_b,
    lengths,
    g_out,
    chain_out,
    msg_out,
    pack_out,
):
    batch, states = f1.shape
    summed = own[...]
    for r in (r1, r2, r3):
        summed = summed + r[...].astype(F32)
    restart = jax.nn.sigmoid(logit[...])
    p = prior[...]
    e = emit[...]
    length = column(lengths[...])
    g = e[2 * batch : 3 * batch] * summed[:batch]
    g_out[...] = g
    chain = e[3 * batch :] * summed[batch:]
    chain_out[...] = chain
    u = (g * (1.0 - restart) * inv[...]).astype(BF16)
    msg_out[:, :states] = u
    last = row_sum(u.astype(F32) * (back_a[:, :states] + back_b[:, states:]))
    h2 = p * e[2 * batch : 3 * batch]
    main = jnp.where(length == 1, p * e[:batch], jnp.where(length == 2, f1[...], g))
    side = jnp.where(length == 3, h2, chain)
    packed = lane_pack(
        [
            lane_pick(part[...], 1),
            row_sum(g * restart),
            row_sum(h2 * restart),
            jnp.where(length < 4, row_sum(main), last),
            jnp.where(length >= 3, row_sum(side), 0.0),
            jnp.where(length >= 4, row_sum(p * e[3 * batch :]), 0.0),
        ],
        batch,
    )
    msg_out[:, states:] = split(packed)
    pack_out[...] = packed


def clean(packed):
    lane = lax.broadcasted_iota(jnp.int32, packed.shape, 1)
    return jnp.where(lane < 6, packed, 0.0)


def totals_kernel(msg_sib, pack, other_a, other_b, out):
    states = msg_sib.shape[1] - 128
    here = pack[...] + joined(msg_sib[:, states:])
    out[...] = clean(here + (other_a[...] + other_b[...]))


def attach_kernel(total, s1, s2, s3, o1, o2, o3):
    states = s1.shape[1] - 128
    parts = split(total[...])
    for out in (o1, o2, o3):
        out[:, states:] = parts


def attach_sum_kernel(msg_sib, pack, other_a, other_b, s1, s2, s3, total, o1, o2, o3):
    totals_kernel(msg_sib, pack, other_a, other_b, total)
    attach_kernel(total, s1, s2, s3, o1, o2, o3)


def finish_kernel(
    own, r1, r2, r3, totals, emit, prior, f1, g2, chain, part, lengths, scaled_out, like_out
):
    batch, states = own.shape
    summed = own[...]
    total = totals[...]
    for r in (r1, r2, r3):
        summed = summed + r[:, :states].astype(F32)
        total = total + joined(r[:, states:])
    p = prior[...]
    e = emit[...]
    length = column(lengths[...])
    z = lane_pick(part[...], 0)
    mass1 = lane_pick(total, 0) / z
    mass2 = (lane_pick(total, 1) + mass1 * lane_pick(total, 2)) / z
    full = lane_pick(total, 3) + mass1 * lane_pick(total, 4) + mass2 * lane_pick(total, 5)
    f2 = g2[...] + mass1 * (p * e[2 * batch : 3 * batch])
    f3 = e[3 * batch :] * (summed + p * mass2) + mass1 * chain[...]
    values = jnp.where(
        length == 1,
        p * e[:batch],
        jnp.where(length == 2, f1[...], jnp.where(length == 3, f2, f3)),
    )
    scaled_out[...] = values / full
    like = jnp.log(full) - jnp.log(z) - length * math.log(EMIT_SCALE)
    diagonal = lax.broadcasted_iota(jnp.int32, (batch, batch), 0) == lax.broadcasted_iota(
        jnp.int32, (batch, batch), 1
    )
    like_out[...] = jnp.sum(jnp.where(diagonal, like, 0.0), axis=0, keepdims=True)


def per_device(
    state_emb,
    from_weight,
    to_weight,
    emit_weight,
    code_emb,
    init_vec,
    restart_logit,
    block_mask,
    codes,
    lengths,
):
    states, width = state_emb.shape
    vocab = code_emb.shape[0]
    cluster = block_mask.shape[1]
    batch, steps = codes.shape
    cols = lax.axis_size("col")
    logit = restart_logit.reshape(1, states)
    length_row = lengths.reshape(1, batch)
    square = shape((states, width), BF16)
    plane = shape((batch, states), F32)
    lanes = shape((batch, 128), F32)
    half_plane = shape((batch, states), BF16)
    message = shape((batch, states + 128), BF16)

    half = states // 2
    half_block = shape((half, width), BF16)
    top, bottom = call(
        halves_kernel,
        (half_block, half_block),
        "halves",
        hbm=(0,),
        micros=6,
        scratch=[pltpu.SemaphoreType.DMA((2,))],
    )(state_emb)
    y_bottom = across(bottom, 2)
    z_top = across(top, 4)
    y_top = across(top, 2)
    z_bottom = across(bottom, 4)

    sib = across(state_emb, 1)
    prior, emit, msg, mass_own = call(
        lambda *refs: emission_kernel(512, *refs),
        (
            shape((1, states), F32),
            shape((batch * steps, states), F32),
            shape((2 * batch, states + 128), F32),
            lanes,
        ),
        "emission",
        hbm=(5, 6),
        micros=0.5,
        scratch=[
            pltpu.VMEM((batch * steps, vocab), BF16),
            pltpu.VMEM((width,), BF16),
            pltpu.VMEM((steps, batch), jnp.int32),
            pltpu.SemaphoreType.DMA((2,)),
        ],
    )(top, bottom, emit_weight, code_emb, logit, init_vec, codes.T)

    scale = 2.0 / math.sqrt(width)
    sums_shape = shape((2 * states, 128), F32)
    wt_shape = shape((2 * states, states), BF16)
    from_own, from_sib, w0, sums0 = call(
        lambda *refs: sources_kernel(scale, *refs),
        (square, square, wt_shape, sums_shape),
        "sources",
        micros=1.5,
    )(block_mask.T, to_weight, top, bottom, sib, from_weight)
    d_top = across(z_top, 2)
    d_bottom = across(y_bottom, 4)
    y_top, z_bottom, sums0 = lax.optimization_barrier((y_top, z_bottom, sums0))
    msg, mass_own, *_ = lax.optimization_barrier((msg, mass_own, y_top, z_bottom))
    msg_sib = across(msg, 1)
    w1, w2, sums1 = call(
        lambda *refs: weights_kernel(scale, (2, 4), *refs),
        (wt_shape, wt_shape, sums_shape),
        "weights",
        micros=2,
    )(block_mask.T, to_weight, from_own, from_sib, y_top, y_bottom, z_top, z_bottom, sums0)
    mass = mass_own + msg_sib[:batch, states:]
    apart = cluster
    while apart < cols:
        mass = mass + across(mass, apart)
        apart *= 2
    w3, row_sums = call(
        lambda *refs: weights_kernel(scale, (6,), *refs),
        (wt_shape, shape((1, 2 * states), F32)),
        "weights",
        micros=1.5,
    )(block_mask.T, to_weight, from_own, from_sib, d_top, d_bottom, sums1)
    wts = (w0, w3, w1, w2)
    row_sums_sib = across(row_sums, 1)

    out = call(
        first_kernel,
        (plane,)
        + (shape((2 * batch, states + 128), BF16),) * 3
        + (shape((1, states), F32), shape((batch, 2 * states), BF16)),
        "first",
        micros=1,
    )(msg, msg_sib, row_sums, row_sums_sib, mass, emit, *wts)
    own, sends, inv, u_chain = out[0], out[1:4], out[4], out[5]
    received = [across(s, shift) for shift, s in zip(SHIFTS, sends)]
    f1, u1, part = call(combine_first_kernel, (plane, half_plane, lanes), "combine_first")(
        own, *received, mass, emit, prior, logit, inv
    )
    u1_sib = across(u1, 1)
    held, _ = lax.optimization_barrier((tuple(received), u1))
    back = call(backward_kernel, shape((batch, 2 * states), F32), "backward", micros=1)(emit, *held, *wts)
    own, *sends = call(
        second_kernel,
        (shape((2 * batch, states), F32),) + (shape((2 * batch, states), BF16),) * 3,
        "second",
        micros=1,
    )(u1, u1_sib, u_chain, *wts)
    back_sib = across(back, 1)
    received = [across(s, shift) for shift, s in zip(SHIFTS, sends)]
    g2, chain, msg2, pack = call(combine_kernel, (plane, plane, message, lanes), "combine")(
        own,
        *received,
        emit,
        prior,
        logit,
        inv,
        f1,
        part,
        back,
        back_sib,
        length_row,
    )
    msg2_sib = across(msg2, 1)
    others = [across(pack, cluster), across(pack, cluster + 1)]
    own, *sends = call(third_kernel, (plane,) + (message,) * 3, "third", micros=1)(
        msg2, msg2_sib, *wts
    )
    if cols == 2 * cluster:
        totals, *sends = call(
            attach_sum_kernel, (lanes,) + (message,) * 3, "attach", aliases={4: 1, 5: 2, 6: 3}
        )(msg2_sib, pack, *others, *sends)
    else:
        totals = call(totals_kernel, lanes, "totals")(msg2_sib, pack, *others)
        apart = 2 * cluster
        while apart < cols:
            totals = totals + across(totals, apart)
            apart *= 2
        sends = call(attach_kernel, (message,) * 3, "attach", aliases={1: 0, 2: 1, 3: 2})(
            totals, *sends
        )
    received = [across(s, shift) for shift, s in zip(SHIFTS, sends)]
    scaled, like = call(finish_kernel, (plane, shape((1, batch), F32)), "finish")(
        own, *received, totals, emit, prior, f1, g2, chain, part, length_row
    )
    return scaled, like.reshape(batch)


def solution(mesh):
    in_specs = (P("col", None), P(), P(), P(), P(), P(), P("col"), P(), P("grp", None), P("grp"))
    out_specs = (P("grp", "col"), P("grp"))
    return jax.shard_map(
        per_device, mesh=mesh, in_specs=in_specs, out_specs=out_specs, check_vma=False
    )
```

```python
import math

import jax
import jax.numpy as jnp
from jax import lax
from jax.experimental import pallas as pl
from jax.experimental.pallas import tpu as pltpu
from jax.sharding import PartitionSpec as P

SOFT_CAP = 10.0
EMIT_SCALE = 2.0**20
SHIFTS = (6, 2, 4)
F32 = jnp.float32
BF16 = jnp.bfloat16
NT = (((1,), (1,)), ((), ()))
NN = (((1,), (0,)), ((), ()))


def dot(lhs, rhs, dims):
    return lax.dot_general(lhs, rhs, dims, preferred_element_type=F32)


def across(shard, apart, axis="col"):
    return lax.ppermute(shard, axis, [(i, i ^ apart) for i in range(lax.axis_size(axis))])


def call(body, out_shape, name, hbm=(), scratch=(), limit=32, aliases=None, micros=0.2):
    def run(*args):
        def space(k):
            return pltpu.HBM if k in hbm else pltpu.VMEM

        return pl.pallas_call(
            body,
            out_shape=out_shape,
            in_specs=[pl.BlockSpec(memory_space=space(k)) for k in range(len(args))],
            out_specs=jax.tree.map(lambda s: pl.BlockSpec(memory_space=pltpu.VMEM), out_shape),
            scratch_shapes=scratch,
            input_output_aliases=aliases or {},
            name=name,
            cost_estimate=pl.CostEstimate(
                flops=int(micros * 1e9), bytes_accessed=int(micros * 3e6), transcendentals=0
            ),
            compiler_params=pltpu.CompilerParams(vmem_limit_bytes=limit << 20),
        )(
            *(
                pltpu.with_memory_space_constraint(arg, pltpu.HBM) if k in hbm else arg
                for k, arg in enumerate(args)
            )
        )

    return run


def shape(dims, dtype):
    return jax.ShapeDtypeStruct(dims, dtype)


def capped_exp(values, scale):
    return jnp.exp2((SOFT_CAP / math.log(2.0)) * jnp.tanh(values * (scale / SOFT_CAP)))


def halves_kernel(emb_hbm, top, bottom, sem):
    half = top.shape[0]
    copies = [
        pltpu.make_async_copy(emb_hbm.at[pl.ds(half, half)], bottom, sem.at[0]),
        pltpu.make_async_copy(emb_hbm.at[pl.ds(0, half)], top, sem.at[1]),
    ]
    for copy in copies:
        copy.start()
    for copy in copies:
        copy.wait()


def emission_kernel(
    tile,
    top,
    bottom,
    emit_w,
    code,
    logit,
    init_hbm,
    ids_hbm,
    prior_out,
    emit_out,
    msg_out,
    mass_out,
    one_hot,
    init_vec,
    codes,
    sem,
):
    copies = [
        pltpu.make_async_copy(init_hbm, init_vec, sem.at[0]),
        pltpu.make_async_copy(ids_hbm, codes, sem.at[1]),
    ]
    for copy in copies:
        copy.start()
    emb = jnp.concatenate([top[...], bottom[...]], axis=0)
    query = dot(emb, emit_w[...], NN).astype(BF16)
    states = emb.shape[0]
    tiles = code.shape[0] // tile
    total = jnp.zeros((8, states), F32)
    for k in range(tiles):
        weights = capped_exp(dot(code[k * tile : (k + 1) * tile, :], query, NT), 3.0)
        total = total + jnp.sum(weights.reshape(tile // 8, 8, states), axis=0)
    for copy in copies:
        copy.wait()
    prior = dot(jnp.broadcast_to(init_vec[...].reshape(1, -1), (8, emb.shape[1])), emb, NT)
    p = capped_exp(prior, 2.0)[:1]
    prior_out[...] = p
    steps, batch = codes.shape
    ids = jnp.concatenate([column(codes[t : t + 1, :]) for t in range(steps)], axis=0)
    lanes = lax.broadcasted_iota(jnp.int32, (batch * steps, tile), 1).astype(F32)
    for k in range(tiles):
        hit = lanes == ids - float(k * tile)
        one_hot[:, k * tile : (k + 1) * tile] = jnp.where(hit, 1.0, 0.0).astype(BF16)
    rows = dot(one_hot[...], code[...], NN)
    factor = EMIT_SCALE / jnp.sum(total, axis=0, keepdims=True)
    emit = capped_exp(dot(rows.astype(BF16), query, NT), 3.0) * factor
    emit_out[...] = emit
    restart = jax.nn.sigmoid(logit[...])
    first = p * emit[:batch]
    third = p * emit[2 * batch : 3 * batch]
    msg_out[:batch, :states] = first * (1.0 - restart)
    msg_out[batch:, :states] = third * (1.0 - restart)
    mass = row_sum(first * restart)
    packed = lane_pack([mass, jnp.broadcast_to(row_sum(p), mass.shape)], batch)
    msg_out[:batch, states:] = packed
    msg_out[batch:, states:] = jnp.zeros((batch, 128), F32)
    mass_out[...] = packed


def column(row):
    count = row.shape[1]
    at_row = lax.broadcasted_iota(jnp.int32, (count, count), 0)
    at_lane = lax.broadcasted_iota(jnp.int32, (count, count), 1)
    return row_sum(jnp.where(at_row == at_lane, row.astype(F32), 0.0))


def lane_pack(columns, rows):
    lane = lax.broadcasted_iota(jnp.int32, (rows, 128), 1)
    packed = jnp.zeros((rows, 128), F32)
    for k, column in enumerate(columns):
        packed = jnp.where(lane == k, column, packed)
    return packed


def lane_pick(packed, k):
    lane = lax.broadcasted_iota(jnp.int32, packed.shape, 1)
    return jnp.sum(jnp.where(lane == k, packed, 0.0), axis=1, keepdims=True)


def split(packed):
    high = packed.astype(BF16).astype(F32)
    rest = packed - high
    middle = rest.astype(BF16).astype(F32)
    return (high + pltpu.roll(middle, 32, 1) + pltpu.roll(rest - middle, 64, 1)).astype(BF16)


def joined(parts):
    parts = parts.astype(F32)
    return parts + pltpu.roll(parts, 96, 1) + pltpu.roll(parts, 64, 1)


def row_sum(values):
    return jnp.sum(values, axis=1, keepdims=True)


def sources_kernel(scale, mask, to_w, top, bottom, sib, from_w, from_a, from_b, out, sum_out):
    half = top.shape[0]
    from_a[:half, :] = dot(top[...], from_w[...], NN).astype(BF16)
    from_a[half:, :] = dot(bottom[...], from_w[...], NN).astype(BF16)
    from_b[...] = dot(sib[...], from_w[...], NN).astype(BF16)
    weights_kernel(scale, (0,), mask, to_w, from_a, from_b, top, bottom, out, sum_out)


def weights_kernel(scale, shifts, mask, to_w, from_a, from_b, *refs):
    states = from_a.shape[0]
    count = len(shifts)
    blocks, outs = refs[: 2 * count], refs[len(refs) - count - 1 : -1]
    before, sum_out = refs[2 * count : len(refs) - count - 1], refs[-1]
    place = lax.rem(lax.axis_index("col"), mask.shape[0])
    at_place = lax.broadcasted_iota(jnp.int32, mask.shape, 0)
    at_col = lax.broadcasted_iota(jnp.int32, mask.shape, 1)
    tile = states // 2
    targets = [dot(block[...], to_w[...], NN).astype(BF16) for block in blocks]
    for side, source in ((0, from_a), (1, from_b)):
        rows = slice(side * states, (side + 1) * states)
        sums = before[0][rows, :] if before else jnp.zeros((states, 128), F32)
        for n, (shift, out) in enumerate(zip(shifts, outs)):
            row = lax.axis_index("col") ^ shift
            keep = (at_place == place ^ side) & (at_col == row)
            keep = jnp.sum(jnp.where(keep, mask[...], 0).astype(F32), axis=(0, 1), keepdims=True)
            for k in range(2):
                target = targets[2 * n + k]
                weights = capped_exp(dot(source[...], target, NT), scale) * keep
                out[rows, k * tile : (k + 1) * tile] = weights.astype(BF16)
                for lane in range(0, tile, 128):
                    sums = sums + weights[:, lane : lane + 128]
        if sum_out.shape[0] == 1:
            sum_out[:, rows] = jnp.sum(sums.T, axis=0, keepdims=True)
        else:
            sum_out[rows, :] = sums


def first_kernel(
    msg_a, msg_b, sums_own, sums_sib, mass, emit, w0, w1, w2, w3, own, s1, s2, s3, inv_out, u_out
):
    states = w0.shape[1]
    batch = mass.shape[0]
    inv_a = 1.0 / (sums_own[:, :states] + sums_sib[:, states:])
    inv_b = 1.0 / (sums_own[:, states:] + sums_sib[:, :states])
    inv_out[...] = inv_a
    u_a = (msg_a[:, :states] * inv_a).astype(BF16)
    u_b = (msg_b[:, :states] * inv_b).astype(BF16)
    u = jnp.concatenate([u_a, u_b], axis=1)
    u_out[...] = u[batch:]
    u = u[:batch]
    own[...] = dot(u, w0[...], NN)
    parts = split(mass[...])
    last = emit[3 * batch :].astype(BF16)
    for w, s in ((w1, s1), (w2, s2), (w3, s3)):
        s[:batch, :states] = dot(u, w[...], NN).astype(BF16)
        s[batch:, :states] = last
        s[:batch, states:] = parts
        s[batch:, states:] = jnp.zeros((batch, 128), BF16)


def combine_first_kernel(own, r1, r2, r3, mass, emit, prior, logit, inv, f_out, u_out, part_out):
    batch, states = own.shape
    summed = own[...]
    total = mass[...]
    for r in (r1, r2, r3):
        summed = summed + r[:batch, :states].astype(F32)
        total = total + joined(r[:batch, states:])
    norm = lane_pick(total, 1)
    ratio = lane_pick(total, 0) / norm
    restart = jax.nn.sigmoid(logit[...])
    f = emit[batch : 2 * batch] * (summed + prior[...] * ratio)
    f_out[...] = f
    u_out[...] = (f * (1.0 - restart) * inv[...]).astype(BF16)
    part_out[...] = lane_pack([norm, row_sum(f * restart)], batch)


def backward_kernel(emit, r1, r2, r3, w0, w1, w2, w3, own_out, sib_out):
    states = w0.shape[1]
    batch = own_out.shape[0]
    acc = dot(emit[3 * batch :].astype(BF16), w0[...], NT)
    for r, w in ((r1, w1), (r2, w2), (r3, w3)):
        acc = acc + dot(r[batch:, :states], w[...], NT)
    own_out[...] = acc[:, :states]
    sib_out[...] = acc[:, states:]


def second_kernel(u_a, u_b, u_chain, w0, w1, w2, w3, own, s1, s2, s3):
    u = jnp.concatenate([jnp.concatenate([u_a[...], u_b[...]], axis=1), u_chain[...]], axis=0)
    own[...] = dot(u, w0[...], NN)
    for w, s in ((w1, s1), (w2, s2), (w3, s3)):
        s[...] = dot(u, w[...], NN).astype(BF16)


def third_kernel(u_a, u_b, w0, w1, w2, w3, own, s1, s2, s3):
    states = w0.shape[1]
    u = jnp.concatenate([u_a[:, :states], u_b[:, :states]], axis=1)
    own[...] = dot(u, w0[...], NN)
    for w, s in ((w1, s1), (w2, s2), (w3, s3)):
        s[:, :states] = dot(u, w[...], NN).astype(BF16)


def combine_kernel(
    own,
    r1,
    r2,
    r3,
    emit,
    prior,
    logit,
    inv,
    f1,
    part,
    back_a,
    back_b,
    lengths,
    g_out,
    chain_out,
    msg_out,
    pack_out,
):
    batch, states = f1.shape
    summed = own[...]
    for r in (r1, r2, r3):
        summed = summed + r[...].astype(F32)
    restart = jax.nn.sigmoid(logit[...])
    p = prior[...]
    e = emit[...]
    length = column(lengths[...])
    g = e[2 * batch : 3 * batch] * summed[:batch]
    g_out[...] = g
    chain = e[3 * batch :] * summed[batch:]
    chain_out[...] = chain
    u = (g * (1.0 - restart) * inv[...]).astype(BF16)
    msg_out[:, :states] = u
    last = row_sum(u.astype(F32) * (back_a[...] + back_b[...]))
    h2 = p * e[2 * batch : 3 * batch]
    main = jnp.where(length == 1, p * e[:batch], jnp.where(length == 2, f1[...], g))
    side = jnp.where(length == 3, h2, chain)
    packed = lane_pack(
        [
            lane_pick(part[...], 1),
            row_sum(g * restart),
            row_sum(h2 * restart),
            jnp.where(length < 4, row_sum(main), last),
            jnp.where(length >= 3, row_sum(side), 0.0),
            jnp.where(length >= 4, row_sum(p * e[3 * batch :]), 0.0),
        ],
        batch,
    )
    msg_out[:, states:] = split(packed)
    pack_out[...] = packed


def clean(packed):
    lane = lax.broadcasted_iota(jnp.int32, packed.shape, 1)
    return jnp.where(lane < 6, packed, 0.0)


def totals_kernel(msg_sib, pack, out):
    states = msg_sib.shape[1] - 128
    out[...] = clean(pack[...] + joined(msg_sib[:, states:]))


def attach_kernel(total, s1, s2, s3, o1, o2, o3):
    states = s1.shape[1] - 128
    parts = split(total[...])
    for out in (o1, o2, o3):
        out[:, states:] = parts


def attach_sum_kernel(here, other, s1, s2, s3, total, o1, o2, o3):
    total[...] = here[...] + other[...]
    attach_kernel(total, s1, s2, s3, o1, o2, o3)


def finish_kernel(
    own, r1, r2, r3, totals, emit, prior, f1, g2, chain, part, lengths, scaled_out, like_out
):
    batch, states = own.shape
    summed = own[...]
    total = totals[...]
    for r in (r1, r2, r3):
        summed = summed + r[:, :states].astype(F32)
        total = total + joined(r[:, states:])
    p = prior[...]
    e = emit[...]
    length = column(lengths[...])
    z = lane_pick(part[...], 0)
    mass1 = lane_pick(total, 0) / z
    mass2 = (lane_pick(total, 1) + mass1 * lane_pick(total, 2)) / z
    full = lane_pick(total, 3) + mass1 * lane_pick(total, 4) + mass2 * lane_pick(total, 5)
    f2 = g2[...] + mass1 * (p * e[2 * batch : 3 * batch])
    f3 = e[3 * batch :] * (summed + p * mass2) + mass1 * chain[...]
    values = jnp.where(
        length == 1,
        p * e[:batch],
        jnp.where(length == 2, f1[...], jnp.where(length == 3, f2, f3)),
    )
    scaled_out[...] = values / full
    like = jnp.log(full) - jnp.log(z) - length * math.log(EMIT_SCALE)
    diagonal = lax.broadcasted_iota(jnp.int32, (batch, batch), 0) == lax.broadcasted_iota(
        jnp.int32, (batch, batch), 1
    )
    like_out[...] = jnp.sum(jnp.where(diagonal, like, 0.0), axis=0, keepdims=True)


def per_device(
    state_emb,
    from_weight,
    to_weight,
    emit_weight,
    code_emb,
    init_vec,
    restart_logit,
    block_mask,
    codes,
    lengths,
):
    states, width = state_emb.shape
    vocab = code_emb.shape[0]
    cluster = block_mask.shape[1]
    batch, steps = codes.shape
    cols = lax.axis_size("col")
    logit = restart_logit.reshape(1, states)
    length_row = lengths.reshape(1, batch)
    square = shape((states, width), BF16)
    plane = shape((batch, states), F32)
    lanes = shape((batch, 128), F32)
    half_plane = shape((batch, states), BF16)
    message = shape((batch, states + 128), BF16)

    half = states // 2
    half_block = shape((half, width), BF16)
    top, bottom = call(
        halves_kernel,
        (half_block, half_block),
        "halves",
        hbm=(0,),
        micros=6,
        scratch=[pltpu.SemaphoreType.DMA((2,))],
    )(state_emb)
    y_bottom = across(bottom, 2)
    z_top = across(top, 4)
    y_top = across(top, 2)
    z_bottom = across(bottom, 4)

    sib = across(state_emb, 1)
    prior, emit, msg, mass_own = call(
        lambda *refs: emission_kernel(512, *refs),
        (
            shape((1, states), F32),
            shape((batch * steps, states), F32),
            shape((2 * batch, states + 128), F32),
            lanes,
        ),
        "emission",
        hbm=(5, 6),
        micros=0.5,
        scratch=[
            pltpu.VMEM((batch * steps, vocab), BF16),
            pltpu.VMEM((width,), BF16),
            pltpu.VMEM((steps, batch), jnp.int32),
            pltpu.SemaphoreType.DMA((2,)),
        ],
    )(top, bottom, emit_weight, code_emb, logit, init_vec, codes.T)

    scale = 2.0 / math.sqrt(width)
    sums_shape = shape((2 * states, 128), F32)
    wt_shape = shape((2 * states, states), BF16)
    from_own, from_sib, w0, sums0 = call(
        lambda *refs: sources_kernel(scale, *refs),
        (square, square, wt_shape, sums_shape),
        "sources",
        micros=1.5,
    )(block_mask.T, to_weight, top, bottom, sib, from_weight)
    d_top = across(z_top, 2)
    d_bottom = across(y_bottom, 4)
    y_top, z_bottom, sums0 = lax.optimization_barrier((y_top, z_bottom, sums0))
    msg, mass_own, *_ = lax.optimization_barrier((msg, mass_own, y_top, z_bottom))
    msg_sib = across(msg, 1)
    w1, w2, sums1 = call(
        lambda *refs: weights_kernel(scale, (2, 4), *refs),
        (wt_shape, wt_shape, sums_shape),
        "weights",
        micros=2,
    )(block_mask.T, to_weight, from_own, from_sib, y_top, y_bottom, z_top, z_bottom, sums0)
    mass = mass_own + msg_sib[:batch, states:]
    apart = cluster
    while apart < cols:
        mass = mass + across(mass, apart)
        apart *= 2
    w3, row_sums = call(
        lambda *refs: weights_kernel(scale, (6,), *refs),
        (wt_shape, shape((1, 2 * states), F32)),
        "weights",
        micros=1.5,
    )(block_mask.T, to_weight, from_own, from_sib, d_top, d_bottom, sums1)
    wts = (w0, w3, w1, w2)
    row_sums_sib = across(row_sums, 1)

    out = call(
        first_kernel,
        (plane,)
        + (shape((2 * batch, states + 128), BF16),) * 3
        + (shape((1, states), F32), shape((batch, 2 * states), BF16)),
        "first",
        micros=1,
    )(msg, msg_sib, row_sums, row_sums_sib, mass, emit, *wts)
    own, sends, inv, u_chain = out[0], out[1:4], out[4], out[5]
    received = [across(s, shift) for shift, s in zip(SHIFTS, sends)]
    f1, u1, part = call(combine_first_kernel, (plane, half_plane, lanes), "combine_first")(
        own, *received, mass, emit, prior, logit, inv
    )
    u1_sib = across(u1, 1)
    held, _ = lax.optimization_barrier((tuple(received), u1))
    back, back_sib = call(backward_kernel, (plane, plane), "backward", micros=1)(
        emit, *held, *wts
    )
    own, *sends = call(
        second_kernel,
        (shape((2 * batch, states), F32),) + (shape((2 * batch, states), BF16),) * 3,
        "second",
        micros=1,
    )(u1, u1_sib, u_chain, *wts)
    back_sib, own = lax.optimization_barrier((back_sib, own))
    back_sib = across(back_sib, 1)
    received = [across(s, shift) for shift, s in zip(SHIFTS, sends)]
    g2, chain, msg2, pack = call(combine_kernel, (plane, plane, message, lanes), "combine")(
        own,
        *received,
        emit,
        prior,
        logit,
        inv,
        f1,
        part,
        back,
        back_sib,
        length_row,
    )
    msg2_sib = across(msg2, 1)
    totals = call(totals_kernel, lanes, "totals")(msg2_sib, pack)
    own, *sends = call(third_kernel, (plane,) + (message,) * 3, "third", micros=1)(
        msg2, msg2_sib, *wts
    )
    other = across(totals, cluster)
    apart = 2 * cluster
    if cols == 2 * cluster:
        totals, *sends = call(
            attach_sum_kernel, (lanes,) + (message,) * 3, "attach", aliases={2: 1, 3: 2, 4: 3}
        )(totals, other, *sends)
    else:
        totals = totals + other
        while apart < cols:
            totals = totals + across(totals, apart)
            apart *= 2
        sends = call(attach_kernel, (message,) * 3, "attach", aliases={1: 0, 2: 1, 3: 2})(
            totals, *sends
        )
    received = [across(s, shift) for shift, s in zip(SHIFTS, sends)]
    scaled, like = call(finish_kernel, (plane, shape((1, batch), F32)), "finish")(
        own, *received, totals, emit, prior, f1, g2, chain, part, length_row
    )
    return scaled, like.reshape(batch)


def solution(mesh):
    in_specs = (P("col", None), P(), P(), P(), P(), P(), P("col"), P(), P("grp", None), P("grp"))
    out_specs = (P("grp", "col"), P("grp"))
    return jax.shard_map(
        per_device, mesh=mesh, in_specs=in_specs, out_specs=out_specs, check_vma=False
    )
```

```python
import math

import jax
import jax.numpy as jnp
from jax import lax
from jax.experimental import pallas as pl
from jax.experimental.pallas import tpu as pltpu
from jax.sharding import PartitionSpec as P

SOFT_CAP = 10.0
EMIT_SCALE = 2.0**20
SHIFTS = (6, 2, 4)
F32 = jnp.float32
BF16 = jnp.bfloat16
NT = (((1,), (1,)), ((), ()))
NN = (((1,), (0,)), ((), ()))


def dot(lhs, rhs, dims):
    return lax.dot_general(lhs, rhs, dims, preferred_element_type=F32)


def across(shard, apart, axis="col"):
    return lax.ppermute(shard, axis, [(i, i ^ apart) for i in range(lax.axis_size(axis))])


def call(body, out_shape, name, hbm=(), scratch=(), limit=32, aliases=None, micros=0.2):
    def run(*args):
        def space(k):
            return pltpu.HBM if k in hbm else pltpu.VMEM

        return pl.pallas_call(
            body,
            out_shape=out_shape,
            in_specs=[pl.BlockSpec(memory_space=space(k)) for k in range(len(args))],
            out_specs=jax.tree.map(lambda s: pl.BlockSpec(memory_space=pltpu.VMEM), out_shape),
            scratch_shapes=scratch,
            input_output_aliases=aliases or {},
            name=name,
            cost_estimate=pl.CostEstimate(
                flops=int(micros * 1e9), bytes_accessed=int(micros * 3e6), transcendentals=0
            ),
            compiler_params=pltpu.CompilerParams(vmem_limit_bytes=limit << 20),
        )(
            *(
                pltpu.with_memory_space_constraint(arg, pltpu.HBM) if k in hbm else arg
                for k, arg in enumerate(args)
            )
        )

    return run


def shape(dims, dtype):
    return jax.ShapeDtypeStruct(dims, dtype)


def capped_exp(values, scale):
    return jnp.exp2((SOFT_CAP / math.log(2.0)) * jnp.tanh(values * (scale / SOFT_CAP)))


def halves_kernel(emb_hbm, top, bottom, sem):
    half = top.shape[0]
    copies = [
        pltpu.make_async_copy(emb_hbm.at[pl.ds(half, half)], bottom, sem.at[0]),
        pltpu.make_async_copy(emb_hbm.at[pl.ds(0, half)], top, sem.at[1]),
    ]
    for copy in copies:
        copy.start()
    for copy in copies:
        copy.wait()


def emission_kernel(
    tile,
    top,
    bottom,
    emit_w,
    code,
    logit,
    init_hbm,
    ids_hbm,
    prior_out,
    emit_out,
    msg_out,
    mass_out,
    one_hot,
    init_vec,
    codes,
    sem,
):
    copies = [
        pltpu.make_async_copy(init_hbm, init_vec, sem.at[0]),
        pltpu.make_async_copy(ids_hbm, codes, sem.at[1]),
    ]
    for copy in copies:
        copy.start()
    emb = jnp.concatenate([top[...], bottom[...]], axis=0)
    query = dot(emb, emit_w[...], NN).astype(BF16)
    states = emb.shape[0]
    tiles = code.shape[0] // tile
    total = jnp.zeros((8, states), F32)
    for k in range(tiles):
        weights = capped_exp(dot(code[k * tile : (k + 1) * tile, :], query, NT), 3.0)
        total = total + jnp.sum(weights.reshape(tile // 8, 8, states), axis=0)
    for copy in copies:
        copy.wait()
    prior = dot(jnp.broadcast_to(init_vec[...].reshape(1, -1), (8, emb.shape[1])), emb, NT)
    p = capped_exp(prior, 2.0)[:1]
    prior_out[...] = p
    steps, batch = codes.shape
    ids = jnp.concatenate([column(codes[t : t + 1, :]) for t in range(steps)], axis=0)
    lanes = lax.broadcasted_iota(jnp.int32, (batch * steps, tile), 1).astype(F32)
    for k in range(tiles):
        hit = lanes == ids - float(k * tile)
        one_hot[:, k * tile : (k + 1) * tile] = jnp.where(hit, 1.0, 0.0).astype(BF16)
    rows = dot(one_hot[...], code[...], NN)
    factor = EMIT_SCALE / jnp.sum(total, axis=0, keepdims=True)
    emit = capped_exp(dot(rows.astype(BF16), query, NT), 3.0) * factor
    emit_out[...] = emit
    restart = jax.nn.sigmoid(logit[...])
    first = p * emit[:batch]
    third = p * emit[2 * batch : 3 * batch]
    msg_out[:batch, :states] = first * (1.0 - restart)
    msg_out[batch:, :states] = third * (1.0 - restart)
    mass = row_sum(first * restart)
    packed = lane_pack([mass, jnp.broadcast_to(row_sum(p), mass.shape)], batch)
    msg_out[:batch, states:] = packed
    msg_out[batch:, states:] = jnp.zeros((batch, 128), F32)
    mass_out[...] = packed


def column(row):
    count = row.shape[1]
    at_row = lax.broadcasted_iota(jnp.int32, (count, count), 0)
    at_lane = lax.broadcasted_iota(jnp.int32, (count, count), 1)
    return row_sum(jnp.where(at_row == at_lane, row.astype(F32), 0.0))


def lane_pack(columns, rows):
    lane = lax.broadcasted_iota(jnp.int32, (rows, 128), 1)
    packed = jnp.zeros((rows, 128), F32)
    for k, column in enumerate(columns):
        packed = jnp.where(lane == k, column, packed)
    return packed


def lane_pick(packed, k):
    lane = lax.broadcasted_iota(jnp.int32, packed.shape, 1)
    return jnp.sum(jnp.where(lane == k, packed, 0.0), axis=1, keepdims=True)


def split(packed):
    high = packed.astype(BF16).astype(F32)
    rest = packed - high
    middle = rest.astype(BF16).astype(F32)
    return (high + pltpu.roll(middle, 32, 1) + pltpu.roll(rest - middle, 64, 1)).astype(BF16)


def joined(parts):
    parts = parts.astype(F32)
    return parts + pltpu.roll(parts, 96, 1) + pltpu.roll(parts, 64, 1)


def row_sum(values):
    return jnp.sum(values, axis=1, keepdims=True)


def sources_kernel(scale, mask, to_w, top, bottom, sib, from_w, from_a, from_b, out, sum_out):
    half = top.shape[0]
    from_a[:half, :] = dot(top[...], from_w[...], NN).astype(BF16)
    from_a[half:, :] = dot(bottom[...], from_w[...], NN).astype(BF16)
    from_b[...] = dot(sib[...], from_w[...], NN).astype(BF16)
    weights_kernel(scale, (0,), mask, to_w, from_a, from_b, top, bottom, out, sum_out)


def weights_kernel(scale, shifts, mask, to_w, from_a, from_b, *refs):
    states = from_a.shape[0]
    count = len(shifts)
    blocks, outs = refs[: 2 * count], refs[len(refs) - count - 1 : -1]
    before, sum_out = refs[2 * count : len(refs) - count - 1], refs[-1]
    place = lax.rem(lax.axis_index("col"), mask.shape[0])
    at_place = lax.broadcasted_iota(jnp.int32, mask.shape, 0)
    at_col = lax.broadcasted_iota(jnp.int32, mask.shape, 1)
    tile = states // 2
    targets = [dot(block[...], to_w[...], NN).astype(BF16) for block in blocks]
    for side, source in ((0, from_a), (1, from_b)):
        rows = slice(side * states, (side + 1) * states)
        sums = before[0][rows, :] if before else jnp.zeros((states, 128), F32)
        for n, (shift, out) in enumerate(zip(shifts, outs)):
            row = lax.axis_index("col") ^ shift
            keep = (at_place == place ^ side) & (at_col == row)
            keep = jnp.sum(jnp.where(keep, mask[...], 0).astype(F32), axis=(0, 1), keepdims=True)
            for k in range(2):
                target = targets[2 * n + k]
                weights = capped_exp(dot(source[...], target, NT), scale) * keep
                out[rows, k * tile : (k + 1) * tile] = weights.astype(BF16)
                for lane in range(0, tile, 128):
                    sums = sums + weights[:, lane : lane + 128]
        if sum_out.shape[0] == 1:
            sum_out[:, rows] = jnp.sum(sums.T, axis=0, keepdims=True)
        else:
            sum_out[rows, :] = sums


def first_kernel(
    msg_a, msg_b, sums_own, sums_sib, mass, emit, w0, w1, w2, w3, own, s1, s2, s3, inv_out, u_out
):
    states = w0.shape[1]
    batch = mass.shape[0]
    inv_a = 1.0 / (sums_own[:, :states] + sums_sib[:, states:])
    inv_b = 1.0 / (sums_own[:, states:] + sums_sib[:, :states])
    inv_out[...] = inv_a
    u_a = (msg_a[:, :states] * inv_a).astype(BF16)
    u_b = (msg_b[:, :states] * inv_b).astype(BF16)
    u = jnp.concatenate([u_a, u_b], axis=1)
    u_out[...] = u[batch:]
    u = u[:batch]
    own[...] = dot(u, w0[...], NN)
    parts = split(mass[...])
    last = emit[3 * batch :].astype(BF16)
    for w, s in ((w1, s1), (w2, s2), (w3, s3)):
        s[:batch, :states] = dot(u, w[...], NN).astype(BF16)
        s[batch:, :states] = last
        s[:batch, states:] = parts
        s[batch:, states:] = jnp.zeros((batch, 128), BF16)


def combine_first_kernel(own, r1, r2, r3, mass, emit, prior, logit, inv, f_out, u_out, part_out):
    batch, states = own.shape
    summed = own[...]
    total = mass[...]
    for r in (r1, r2, r3):
        summed = summed + r[:batch, :states].astype(F32)
        total = total + joined(r[:batch, states:])
    norm = lane_pick(total, 1)
    ratio = lane_pick(total, 0) / norm
    restart = jax.nn.sigmoid(logit[...])
    f = emit[batch : 2 * batch] * (summed + prior[...] * ratio)
    f_out[...] = f
    u_out[...] = (f * (1.0 - restart) * inv[...]).astype(BF16)
    part_out[...] = lane_pack([norm, row_sum(f * restart)], batch)


def backward_kernel(emit, r1, r2, r3, w0, w1, w2, w3, own_out, sib_out):
    states = w0.shape[1]
    batch = own_out.shape[0]
    acc = dot(emit[3 * batch :].astype(BF16), w0[...], NT)
    for r, w in ((r1, w1), (r2, w2), (r3, w3)):
        acc = acc + dot(r[batch:, :states], w[...], NT)
    own_out[...] = acc[:, :states]
    sib_out[...] = acc[:, states:]


def second_kernel(u_a, u_b, u_chain, w0, w1, w2, w3, own, s1, s2, s3):
    u = jnp.concatenate([jnp.concatenate([u_a[...], u_b[...]], axis=1), u_chain[...]], axis=0)
    own[...] = dot(u, w0[...], NN)
    for w, s in ((w1, s1), (w2, s2), (w3, s3)):
        s[...] = dot(u, w[...], NN).astype(BF16)


def third_kernel(u_a, u_b, w0, w1, w2, w3, own, s1, s2, s3):
    states = w0.shape[1]
    u = jnp.concatenate([u_a[:, :states], u_b[:, :states]], axis=1)
    own[...] = dot(u, w0[...], NN)
    for w, s in ((w1, s1), (w2, s2), (w3, s3)):
        s[:, :states] = dot(u, w[...], NN).astype(BF16)


def combine_kernel(
    own,
    r1,
    r2,
    r3,
    emit,
    prior,
    logit,
    inv,
    f1,
    part,
    back_a,
    back_b,
    lengths,
    g_out,
    chain_out,
    msg_out,
    pack_out,
):
    batch, states = f1.shape
    summed = own[...]
    for r in (r1, r2, r3):
        summed = summed + r[...].astype(F32)
    restart = jax.nn.sigmoid(logit[...])
    p = prior[...]
    e = emit[...]
    length = column(lengths[...])
    g = e[2 * batch : 3 * batch] * summed[:batch]
    g_out[...] = g
    chain = e[3 * batch :] * summed[batch:]
    chain_out[...] = chain
    u = (g * (1.0 - restart) * inv[...]).astype(BF16)
    msg_out[:, :states] = u
    last = row_sum(u.astype(F32) * (back_a[...] + back_b[...]))
    h2 = p * e[2 * batch : 3 * batch]
    main = jnp.where(length == 1, p * e[:batch], jnp.where(length == 2, f1[...], g))
    side = jnp.where(length == 3, h2, chain)
    packed = lane_pack(
        [
            lane_pick(part[...], 1),
            row_sum(g * restart),
            row_sum(h2 * restart),
            jnp.where(length < 4, row_sum(main), last),
            jnp.where(length >= 3, row_sum(side), 0.0),
            jnp.where(length >= 4, row_sum(p * e[3 * batch :]), 0.0),
        ],
        batch,
    )
    msg_out[:, states:] = split(packed)
    pack_out[...] = packed


def clean(packed):
    lane = lax.broadcasted_iota(jnp.int32, packed.shape, 1)
    return jnp.where(lane < 6, packed, 0.0)


def totals_kernel(msg_sib, pack, out):
    states = msg_sib.shape[1] - 128
    out[...] = clean(pack[...] + joined(msg_sib[:, states:]))


def attach_kernel(total, s1, s2, s3, o1, o2, o3):
    states = s1.shape[1] - 128
    parts = split(total[...])
    for out in (o1, o2, o3):
        out[:, states:] = parts


def attach_sum_kernel(here, other, s1, s2, s3, total, o1, o2, o3):
    total[...] = here[...] + other[...]
    attach_kernel(total, s1, s2, s3, o1, o2, o3)


def finish_kernel(
    own, r1, r2, r3, totals, emit, prior, f1, g2, chain, part, lengths, scaled_out, like_out
):
    batch, states = own.shape
    summed = own[...]
    total = totals[...]
    for r in (r1, r2, r3):
        summed = summed + r[:, :states].astype(F32)
        total = total + joined(r[:, states:])
    p = prior[...]
    e = emit[...]
    length = column(lengths[...])
    z = lane_pick(part[...], 0)
    mass1 = lane_pick(total, 0) / z
    mass2 = (lane_pick(total, 1) + mass1 * lane_pick(total, 2)) / z
    full = lane_pick(total, 3) + mass1 * lane_pick(total, 4) + mass2 * lane_pick(total, 5)
    f2 = g2[...] + mass1 * (p * e[2 * batch : 3 * batch])
    f3 = e[3 * batch :] * (summed + p * mass2) + mass1 * chain[...]
    values = jnp.where(
        length == 1,
        p * e[:batch],
        jnp.where(length == 2, f1[...], jnp.where(length == 3, f2, f3)),
    )
    scaled_out[...] = values / full
    like = jnp.log(full) - jnp.log(z) - length * math.log(EMIT_SCALE)
    diagonal = lax.broadcasted_iota(jnp.int32, (batch, batch), 0) == lax.broadcasted_iota(
        jnp.int32, (batch, batch), 1
    )
    like_out[...] = jnp.sum(jnp.where(diagonal, like, 0.0), axis=0, keepdims=True)


def per_device(
    state_emb,
    from_weight,
    to_weight,
    emit_weight,
    code_emb,
    init_vec,
    restart_logit,
    block_mask,
    codes,
    lengths,
):
    states, width = state_emb.shape
    vocab = code_emb.shape[0]
    cluster = block_mask.shape[1]
    batch, steps = codes.shape
    cols = lax.axis_size("col")
    logit = restart_logit.reshape(1, states)
    length_row = lengths.reshape(1, batch)
    square = shape((states, width), BF16)
    plane = shape((batch, states), F32)
    lanes = shape((batch, 128), F32)
    half_plane = shape((batch, states), BF16)
    message = shape((batch, states + 128), BF16)

    half = states // 2
    half_block = shape((half, width), BF16)
    top, bottom = call(
        halves_kernel,
        (half_block, half_block),
        "halves",
        hbm=(0,),
        micros=6,
        scratch=[pltpu.SemaphoreType.DMA((2,))],
    )(state_emb)
    y_bottom = across(bottom, 2)
    z_top = across(top, 4)
    y_top = across(top, 2)
    z_bottom = across(bottom, 4)

    sib = across(state_emb, 1)
    prior, emit, msg, mass_own = call(
        lambda *refs: emission_kernel(512, *refs),
        (
            shape((1, states), F32),
            shape((batch * steps, states), F32),
            shape((2 * batch, states + 128), F32),
            lanes,
        ),
        "emission",
        hbm=(5, 6),
        micros=0.5,
        scratch=[
            pltpu.VMEM((batch * steps, vocab), BF16),
            pltpu.VMEM((width,), BF16),
            pltpu.VMEM((steps, batch), jnp.int32),
            pltpu.SemaphoreType.DMA((2,)),
        ],
    )(top, bottom, emit_weight, code_emb, logit, init_vec, codes.T)

    scale = 2.0 / math.sqrt(width)
    sums_shape = shape((2 * states, 128), F32)
    wt_shape = shape((2 * states, states), BF16)
    from_own, from_sib, w0, sums0 = call(
        lambda *refs: sources_kernel(scale, *refs),
        (square, square, wt_shape, sums_shape),
        "sources",
        micros=1.5,
    )(block_mask.T, to_weight, top, bottom, sib, from_weight)
    d_top = across(z_top, 2)
    d_bottom = across(y_bottom, 4)
    y_top, z_bottom, sums0 = lax.optimization_barrier((y_top, z_bottom, sums0))
    msg, mass_own, *_ = lax.optimization_barrier((msg, mass_own, y_top, z_bottom))
    msg_sib = across(msg, 1)
    w1, w2, sums1 = call(
        lambda *refs: weights_kernel(scale, (2, 4), *refs),
        (wt_shape, wt_shape, sums_shape),
        "weights",
        micros=2,
    )(block_mask.T, to_weight, from_own, from_sib, y_top, y_bottom, z_top, z_bottom, sums0)
    mass = mass_own + msg_sib[:batch, states:]
    apart = cluster
    while apart < cols:
        mass = mass + across(mass, apart)
        apart *= 2
    w3, row_sums = call(
        lambda *refs: weights_kernel(scale, (6,), *refs),
        (wt_shape, shape((1, 2 * states), F32)),
        "weights",
        micros=1.5,
    )(block_mask.T, to_weight, from_own, from_sib, d_top, d_bottom, sums1)
    wts = (w0, w3, w1, w2)
    row_sums_sib = across(row_sums, 1)

    out = call(
        first_kernel,
        (plane,)
        + (shape((2 * batch, states + 128), BF16),) * 3
        + (shape((1, states), F32), shape((batch, 2 * states), BF16)),
        "first",
        micros=1,
    )(msg, msg_sib, row_sums, row_sums_sib, mass, emit, *wts)
    own, sends, inv, u_chain = out[0], out[1:4], out[4], out[5]
    received = [across(s, shift) for shift, s in zip(SHIFTS, sends)]
    f1, u1, part = call(combine_first_kernel, (plane, half_plane, lanes), "combine_first")(
        own, *received, mass, emit, prior, logit, inv
    )
    u1_sib = across(u1, 1)
    held, _ = lax.optimization_barrier((tuple(received), u1))
    back, back_sib = call(backward_kernel, (plane, plane), "backward", micros=1)(
        emit, *held, *wts
    )
    back, u_chain = lax.optimization_barrier((back, u_chain))
    own, *sends = call(
        second_kernel,
        (shape((2 * batch, states), F32),) + (shape((2 * batch, states), BF16),) * 3,
        "second",
        micros=1,
    )(u1, u1_sib, u_chain, *wts)
    received = [across(s, shift) for shift, s in zip(SHIFTS, sends)]
    back, back_sib, own, received[0] = lax.optimization_barrier((back, back_sib, own, received[0]))
    back_sib = across(back_sib, 1)
    g2, chain, msg2, pack = call(combine_kernel, (plane, plane, message, lanes), "combine")(
        own,
        *received,
        emit,
        prior,
        logit,
        inv,
        f1,
        part,
        back,
        back_sib,
        length_row,
    )
    msg2_sib = across(msg2, 1)
    totals = call(totals_kernel, lanes, "totals")(msg2_sib, pack)
    own, *sends = call(third_kernel, (plane,) + (message,) * 3, "third", micros=1)(
        msg2, msg2_sib, *wts
    )
    other = across(totals, cluster)
    apart = 2 * cluster
    if cols == 2 * cluster:
        totals, *sends = call(
            attach_sum_kernel, (lanes,) + (message,) * 3, "attach", aliases={2: 1, 3: 2, 4: 3}
        )(totals, other, *sends)
    else:
        totals = totals + other
        while apart < cols:
            totals = totals + across(totals, apart)
            apart *= 2
        sends = call(attach_kernel, (message,) * 3, "attach", aliases={1: 0, 2: 1, 3: 2})(
            totals, *sends
        )
    received = [across(s, shift) for shift, s in zip(SHIFTS, sends)]
    scaled, like = call(finish_kernel, (plane, shape((1, batch), F32)), "finish")(
        own, *received, totals, emit, prior, f1, g2, chain, part, length_row
    )
    return scaled, like.reshape(batch)


def solution(mesh):
    in_specs = (P("col", None), P(), P(), P(), P(), P(), P("col"), P(), P("grp", None), P("grp"))
    out_specs = (P("grp", "col"), P("grp"))
    return jax.shard_map(
        per_device, mesh=mesh, in_specs=in_specs, out_specs=out_specs, check_vma=False
    )
```

```python
import math

import jax
import jax.numpy as jnp
from jax import lax
from jax.experimental import pallas as pl
from jax.experimental.pallas import tpu as pltpu
from jax.sharding import PartitionSpec as P

SOFT_CAP = 10.0
EMIT_SCALE = 2.0**20
SHIFTS = (6, 2, 4)
F32 = jnp.float32
BF16 = jnp.bfloat16
NT = (((1,), (1,)), ((), ()))
NN = (((1,), (0,)), ((), ()))


def dot(lhs, rhs, dims):
    return lax.dot_general(lhs, rhs, dims, preferred_element_type=F32)


def across(shard, apart, axis="col"):
    return lax.ppermute(shard, axis, [(i, i ^ apart) for i in range(lax.axis_size(axis))])


def call(body, out_shape, name, hbm=(), scratch=(), limit=32, aliases=None, micros=0.2):
    def run(*args):
        def space(k):
            return pltpu.HBM if k in hbm else pltpu.VMEM

        return pl.pallas_call(
            body,
            out_shape=out_shape,
            in_specs=[pl.BlockSpec(memory_space=space(k)) for k in range(len(args))],
            out_specs=jax.tree.map(lambda s: pl.BlockSpec(memory_space=pltpu.VMEM), out_shape),
            scratch_shapes=scratch,
            input_output_aliases=aliases or {},
            name=name,
            cost_estimate=pl.CostEstimate(
                flops=int(micros * 1e9), bytes_accessed=int(micros * 3e6), transcendentals=0
            ),
            compiler_params=pltpu.CompilerParams(vmem_limit_bytes=limit << 20),
        )(
            *(
                pltpu.with_memory_space_constraint(arg, pltpu.HBM) if k in hbm else arg
                for k, arg in enumerate(args)
            )
        )

    return run


def shape(dims, dtype):
    return jax.ShapeDtypeStruct(dims, dtype)


def capped_exp(values, scale):
    return jnp.exp2((SOFT_CAP / math.log(2.0)) * jnp.tanh(values * (scale / SOFT_CAP)))


def halves_kernel(emb_hbm, top, bottom, sem):
    half = top.shape[0]
    copies = [
        pltpu.make_async_copy(emb_hbm.at[pl.ds(half, half)], bottom, sem.at[0]),
        pltpu.make_async_copy(emb_hbm.at[pl.ds(0, half)], top, sem.at[1]),
    ]
    for copy in copies:
        copy.start()
    for copy in copies:
        copy.wait()


def emission_kernel(
    tile,
    top,
    bottom,
    emit_w,
    code,
    logit,
    init_hbm,
    ids_hbm,
    prior_out,
    emit_out,
    msg_out,
    mass_out,
    one_hot,
    init_vec,
    codes,
    sem,
):
    copies = [
        pltpu.make_async_copy(init_hbm, init_vec, sem.at[0]),
        pltpu.make_async_copy(ids_hbm, codes, sem.at[1]),
    ]
    for copy in copies:
        copy.start()
    emb = jnp.concatenate([top[...], bottom[...]], axis=0)
    query = dot(emb, emit_w[...], NN).astype(BF16)
    states = emb.shape[0]
    tiles = code.shape[0] // tile
    total = jnp.zeros((8, states), F32)
    for k in range(tiles):
        weights = capped_exp(dot(code[k * tile : (k + 1) * tile, :], query, NT), 3.0)
        total = total + jnp.sum(weights.reshape(tile // 8, 8, states), axis=0)
    for copy in copies:
        copy.wait()
    prior = dot(jnp.broadcast_to(init_vec[...].reshape(1, -1), (8, emb.shape[1])), emb, NT)
    p = capped_exp(prior, 2.0)[:1]
    prior_out[...] = p
    steps, batch = codes.shape
    ids = jnp.concatenate([column(codes[t : t + 1, :]) for t in range(steps)], axis=0)
    lanes = lax.broadcasted_iota(jnp.int32, (batch * steps, tile), 1).astype(F32)
    for k in range(tiles):
        hit = lanes == ids - float(k * tile)
        one_hot[:, k * tile : (k + 1) * tile] = jnp.where(hit, 1.0, 0.0).astype(BF16)
    rows = dot(one_hot[...], code[...], NN)
    factor = EMIT_SCALE / jnp.sum(total, axis=0, keepdims=True)
    emit = capped_exp(dot(rows.astype(BF16), query, NT), 3.0) * factor
    emit_out[...] = emit
    restart = jax.nn.sigmoid(logit[...])
    first = p * emit[:batch]
    third = p * emit[2 * batch : 3 * batch]
    msg_out[:batch, :states] = first * (1.0 - restart)
    msg_out[batch:, :states] = third * (1.0 - restart)
    mass = row_sum(first * restart)
    packed = lane_pack([mass, jnp.broadcast_to(row_sum(p), mass.shape)], batch)
    msg_out[:batch, states:] = packed
    msg_out[batch:, states:] = jnp.zeros((batch, 128), F32)
    mass_out[...] = packed


def column(row):
    count = row.shape[1]
    at_row = lax.broadcasted_iota(jnp.int32, (count, count), 0)
    at_lane = lax.broadcasted_iota(jnp.int32, (count, count), 1)
    return row_sum(jnp.where(at_row == at_lane, row.astype(F32), 0.0))


def lane_pack(columns, rows):
    lane = lax.broadcasted_iota(jnp.int32, (rows, 128), 1)
    packed = jnp.zeros((rows, 128), F32)
    for k, column in enumerate(columns):
        packed = jnp.where(lane == k, column, packed)
    return packed


def lane_pick(packed, k):
    lane = lax.broadcasted_iota(jnp.int32, packed.shape, 1)
    return jnp.sum(jnp.where(lane == k, packed, 0.0), axis=1, keepdims=True)


def split(packed):
    high = packed.astype(BF16).astype(F32)
    rest = packed - high
    middle = rest.astype(BF16).astype(F32)
    return (high + pltpu.roll(middle, 32, 1) + pltpu.roll(rest - middle, 64, 1)).astype(BF16)


def joined(parts):
    parts = parts.astype(F32)
    return parts + pltpu.roll(parts, 96, 1) + pltpu.roll(parts, 64, 1)


def row_sum(values):
    return jnp.sum(values, axis=1, keepdims=True)


def sources_kernel(scale, mask, to_w, top, bottom, sib, from_w, from_a, from_b, out, sum_out):
    half = top.shape[0]
    from_a[:half, :] = dot(top[...], from_w[...], NN).astype(BF16)
    from_a[half:, :] = dot(bottom[...], from_w[...], NN).astype(BF16)
    from_b[...] = dot(sib[...], from_w[...], NN).astype(BF16)
    weights_kernel(scale, (0,), mask, to_w, from_a, from_b, top, bottom, out, sum_out)


def target_kernel(block, to_w, out):
    out[...] = dot(block[...], to_w[...], NN).astype(BF16)


def weights_kernel(scale, shifts, mask, to_w, from_a, from_b, *refs):
    states = from_a.shape[0]
    count = len(shifts)
    blocks, outs = refs[: 2 * count], refs[len(refs) - count - 1 : -1]
    before, sum_out = refs[2 * count : len(refs) - count - 1], refs[-1]
    place = lax.rem(lax.axis_index("col"), mask.shape[0])
    at_place = lax.broadcasted_iota(jnp.int32, mask.shape, 0)
    at_col = lax.broadcasted_iota(jnp.int32, mask.shape, 1)
    tile = states // 2
    if shifts == (6,):
        targets = [block[...] for block in blocks]
    else:
        targets = [dot(block[...], to_w[...], NN).astype(BF16) for block in blocks]
    for side, source in ((0, from_a), (1, from_b)):
        rows = slice(side * states, (side + 1) * states)
        sums = before[0][rows, :] if before else jnp.zeros((states, 128), F32)
        for n, (shift, out) in enumerate(zip(shifts, outs)):
            row = lax.axis_index("col") ^ shift
            keep = (at_place == place ^ side) & (at_col == row)
            keep = jnp.sum(jnp.where(keep, mask[...], 0).astype(F32), axis=(0, 1), keepdims=True)
            for k in range(2):
                target = targets[2 * n + k]
                weights = capped_exp(dot(source[...], target, NT), scale) * keep
                out[rows, k * tile : (k + 1) * tile] = weights.astype(BF16)
                for lane in range(0, tile, 128):
                    sums = sums + weights[:, lane : lane + 128]
        if sum_out.shape[0] == 1:
            sum_out[:, rows] = jnp.sum(sums.T, axis=0, keepdims=True)
        else:
            sum_out[rows, :] = sums


def first_kernel(
    msg_a, msg_b, sums_own, sums_sib, mass, emit, w0, w1, w2, w3, own, s1, s2, s3, inv_out, u_out
):
    states = w0.shape[1]
    batch = mass.shape[0]
    inv_a = 1.0 / (sums_own[:, :states] + sums_sib[:, states:])
    inv_b = 1.0 / (sums_own[:, states:] + sums_sib[:, :states])
    inv_out[...] = inv_a
    u_a = (msg_a[:, :states] * inv_a).astype(BF16)
    u_b = (msg_b[:, :states] * inv_b).astype(BF16)
    u = jnp.concatenate([u_a, u_b], axis=1)
    u_out[...] = u[batch:]
    u = u[:batch]
    own[...] = dot(u, w0[...], NN)
    parts = split(mass[...])
    last = emit[3 * batch :].astype(BF16)
    for w, s in ((w1, s1), (w2, s2), (w3, s3)):
        s[:batch, :states] = dot(u, w[...], NN).astype(BF16)
        s[batch:, :states] = last
        s[:batch, states:] = parts
        s[batch:, states:] = jnp.zeros((batch, 128), BF16)


def combine_first_kernel(own, r1, r2, r3, mass, emit, prior, logit, inv, f_out, u_out, part_out):
    batch, states = own.shape
    summed = own[...]
    total = mass[...]
    for r in (r1, r2, r3):
        summed = summed + r[:batch, :states].astype(F32)
        total = total + joined(r[:batch, states:])
    norm = lane_pick(total, 1)
    ratio = lane_pick(total, 0) / norm
    restart = jax.nn.sigmoid(logit[...])
    f = emit[batch : 2 * batch] * (summed + prior[...] * ratio)
    f_out[...] = f
    u_out[...] = (f * (1.0 - restart) * inv[...]).astype(BF16)
    part_out[...] = lane_pack([norm, row_sum(f * restart)], batch)


def backward_kernel(emit, r1, r2, r3, w0, w1, w2, w3, own_out, sib_out):
    states = w0.shape[1]
    batch = own_out.shape[0]
    acc = dot(emit[3 * batch :].astype(BF16), w0[...], NT)
    for r, w in ((r1, w1), (r2, w2), (r3, w3)):
        acc = acc + dot(r[batch:, :states], w[...], NT)
    own_out[...] = acc[:, :states]
    sib_out[...] = acc[:, states:]


def second_kernel(u_a, u_b, u_chain, w0, w1, w2, w3, own, s1, s2, s3):
    u = jnp.concatenate([jnp.concatenate([u_a[...], u_b[...]], axis=1), u_chain[...]], axis=0)
    own[...] = dot(u, w0[...], NN)
    for w, s in ((w1, s1), (w2, s2), (w3, s3)):
        s[...] = dot(u, w[...], NN).astype(BF16)


def third_kernel(u_a, u_b, w0, w1, w2, w3, own, s1, s2, s3):
    states = w0.shape[1]
    u = jnp.concatenate([u_a[:, :states], u_b[:, :states]], axis=1)
    own[...] = dot(u, w0[...], NN)
    for w, s in ((w1, s1), (w2, s2), (w3, s3)):
        s[:, :states] = dot(u, w[...], NN).astype(BF16)


def combine_kernel(
    own,
    r1,
    r2,
    r3,
    emit,
    prior,
    logit,
    inv,
    f1,
    part,
    back_a,
    back_b,
    lengths,
    g_out,
    chain_out,
    msg_out,
    pack_out,
):
    batch, states = f1.shape
    summed = own[...]
    for r in (r1, r2, r3):
        summed = summed + r[...].astype(F32)
    restart = jax.nn.sigmoid(logit[...])
    p = prior[...]
    e = emit[...]
    length = column(lengths[...])
    g = e[2 * batch : 3 * batch] * summed[:batch]
    g_out[...] = g
    chain = e[3 * batch :] * summed[batch:]
    chain_out[...] = chain
    u = (g * (1.0 - restart) * inv[...]).astype(BF16)
    msg_out[:, :states] = u
    last = row_sum(u.astype(F32) * (back_a[...] + back_b[...]))
    h2 = p * e[2 * batch : 3 * batch]
    main = jnp.where(length == 1, p * e[:batch], jnp.where(length == 2, f1[...], g))
    side = jnp.where(length == 3, h2, chain)
    packed = lane_pack(
        [
            lane_pick(part[...], 1),
            row_sum(g * restart),
            row_sum(h2 * restart),
            jnp.where(length < 4, row_sum(main), last),
            jnp.where(length >= 3, row_sum(side), 0.0),
            jnp.where(length >= 4, row_sum(p * e[3 * batch :]), 0.0),
        ],
        batch,
    )
    msg_out[:, states:] = split(packed)
    pack_out[...] = packed


def clean(packed):
    lane = lax.broadcasted_iota(jnp.int32, packed.shape, 1)
    return jnp.where(lane < 6, packed, 0.0)


def totals_kernel(msg_sib, pack, out):
    states = msg_sib.shape[1] - 128
    out[...] = clean(pack[...] + joined(msg_sib[:, states:]))


def attach_kernel(total, s1, s2, s3, o1, o2, o3):
    states = s1.shape[1] - 128
    parts = split(total[...])
    for out in (o1, o2, o3):
        out[:, states:] = parts


def attach_sum_kernel(here, other, s1, s2, s3, total, o1, o2, o3):
    total[...] = here[...] + other[...]
    attach_kernel(total, s1, s2, s3, o1, o2, o3)


def finish_kernel(
    own, r1, r2, r3, totals, emit, prior, f1, g2, chain, part, lengths, scaled_out, like_out
):
    batch, states = own.shape
    summed = own[...]
    total = totals[...]
    for r in (r1, r2, r3):
        summed = summed + r[:, :states].astype(F32)
        total = total + joined(r[:, states:])
    p = prior[...]
    e = emit[...]
    length = column(lengths[...])
    z = lane_pick(part[...], 0)
    mass1 = lane_pick(total, 0) / z
    mass2 = (lane_pick(total, 1) + mass1 * lane_pick(total, 2)) / z
    full = lane_pick(total, 3) + mass1 * lane_pick(total, 4) + mass2 * lane_pick(total, 5)
    f2 = g2[...] + mass1 * (p * e[2 * batch : 3 * batch])
    f3 = e[3 * batch :] * (summed + p * mass2) + mass1 * chain[...]
    values = jnp.where(
        length == 1,
        p * e[:batch],
        jnp.where(length == 2, f1[...], jnp.where(length == 3, f2, f3)),
    )
    scaled_out[...] = values / full
    like = jnp.log(full) - jnp.log(z) - length * math.log(EMIT_SCALE)
    diagonal = lax.broadcasted_iota(jnp.int32, (batch, batch), 0) == lax.broadcasted_iota(
        jnp.int32, (batch, batch), 1
    )
    like_out[...] = jnp.sum(jnp.where(diagonal, like, 0.0), axis=0, keepdims=True)


def per_device(
    state_emb,
    from_weight,
    to_weight,
    emit_weight,
    code_emb,
    init_vec,
    restart_logit,
    block_mask,
    codes,
    lengths,
):
    states, width = state_emb.shape
    vocab = code_emb.shape[0]
    cluster = block_mask.shape[1]
    batch, steps = codes.shape
    cols = lax.axis_size("col")
    logit = restart_logit.reshape(1, states)
    length_row = lengths.reshape(1, batch)
    square = shape((states, width), BF16)
    plane = shape((batch, states), F32)
    lanes = shape((batch, 128), F32)
    half_plane = shape((batch, states), BF16)
    message = shape((batch, states + 128), BF16)

    half = states // 2
    half_block = shape((half, width), BF16)
    top, bottom = call(
        halves_kernel,
        (half_block, half_block),
        "halves",
        hbm=(0,),
        micros=6,
        scratch=[pltpu.SemaphoreType.DMA((2,))],
    )(state_emb)
    y_bottom = across(bottom, 2)
    z_top = across(top, 4)
    y_top = across(top, 2)
    z_bottom = across(bottom, 4)

    sib = across(state_emb, 1)
    prior, emit, msg, mass_own = call(
        lambda *refs: emission_kernel(512, *refs),
        (
            shape((1, states), F32),
            shape((batch * steps, states), F32),
            shape((2 * batch, states + 128), F32),
            lanes,
        ),
        "emission",
        hbm=(5, 6),
        micros=0.5,
        scratch=[
            pltpu.VMEM((batch * steps, vocab), BF16),
            pltpu.VMEM((width,), BF16),
            pltpu.VMEM((steps, batch), jnp.int32),
            pltpu.SemaphoreType.DMA((2,)),
        ],
    )(top, bottom, emit_weight, code_emb, logit, init_vec, codes.T)

    scale = 2.0 / math.sqrt(width)
    sums_shape = shape((2 * states, 128), F32)
    wt_shape = shape((2 * states, states), BF16)
    from_own, from_sib, w0, sums0 = call(
        lambda *refs: sources_kernel(scale, *refs),
        (square, square, wt_shape, sums_shape),
        "sources",
        micros=1.5,
    )(block_mask.T, to_weight, top, bottom, sib, from_weight)
    d_top = across(call(target_kernel, half_block, "target")(z_top, to_weight), 2)
    d_bottom = across(call(target_kernel, half_block, "target")(y_bottom, to_weight), 4)
    y_top, z_bottom, sums0 = lax.optimization_barrier((y_top, z_bottom, sums0))
    msg, mass_own, *_ = lax.optimization_barrier((msg, mass_own, y_top, z_bottom))
    msg_sib = across(msg, 1)
    w1, w2, sums1 = call(
        lambda *refs: weights_kernel(scale, (2, 4), *refs),
        (wt_shape, wt_shape, sums_shape),
        "weights",
        micros=2,
    )(block_mask.T, to_weight, from_own, from_sib, y_top, y_bottom, z_top, z_bottom, sums0)
    mass = mass_own + msg_sib[:batch, states:]
    apart = cluster
    while apart < cols:
        mass = mass + across(mass, apart)
        apart *= 2
    w3, row_sums = call(
        lambda *refs: weights_kernel(scale, (6,), *refs),
        (wt_shape, shape((1, 2 * states), F32)),
        "weights",
        micros=1.5,
    )(block_mask.T, to_weight, from_own, from_sib, d_top, d_bottom, sums1)
    wts = (w0, w3, w1, w2)
    row_sums_sib = across(row_sums, 1)

    out = call(
        first_kernel,
        (plane,)
        + (shape((2 * batch, states + 128), BF16),) * 3
        + (shape((1, states), F32), shape((batch, 2 * states), BF16)),
        "first",
        micros=1,
    )(msg, msg_sib, row_sums, row_sums_sib, mass, emit, *wts)
    own, sends, inv, u_chain = out[0], out[1:4], out[4], out[5]
    received = [across(s, shift) for shift, s in zip(SHIFTS, sends)]
    f1, u1, part = call(combine_first_kernel, (plane, half_plane, lanes), "combine_first")(
        own, *received, mass, emit, prior, logit, inv
    )
    u1_sib = across(u1, 1)
    held, _ = lax.optimization_barrier((tuple(received), u1))
    back, back_sib = call(backward_kernel, (plane, plane), "backward", micros=1)(
        emit, *held, *wts
    )
    back, u_chain = lax.optimization_barrier((back, u_chain))
    own, *sends = call(
        second_kernel,
        (shape((2 * batch, states), F32),) + (shape((2 * batch, states), BF16),) * 3,
        "second",
        micros=1,
    )(u1, u1_sib, u_chain, *wts)
    received = [across(s, shift) for shift, s in zip(SHIFTS, sends)]
    back, back_sib, own, received[0] = lax.optimization_barrier((back, back_sib, own, received[0]))
    back_sib = across(back_sib, 1)
    g2, chain, msg2, pack = call(combine_kernel, (plane, plane, message, lanes), "combine")(
        own,
        *received,
        emit,
        prior,
        logit,
        inv,
        f1,
        part,
        back,
        back_sib,
        length_row,
    )
    msg2_sib = across(msg2, 1)
    totals = call(totals_kernel, lanes, "totals")(msg2_sib, pack)
    own, *sends = call(third_kernel, (plane,) + (message,) * 3, "third", micros=1)(
        msg2, msg2_sib, *wts
    )
    other = across(totals, cluster)
    apart = 2 * cluster
    if cols == 2 * cluster:
        totals, *sends = call(
            attach_sum_kernel, (lanes,) + (message,) * 3, "attach", aliases={2: 1, 3: 2, 4: 3}
        )(totals, other, *sends)
    else:
        totals = totals + other
        while apart < cols:
            totals = totals + across(totals, apart)
            apart *= 2
        sends = call(attach_kernel, (message,) * 3, "attach", aliases={1: 0, 2: 1, 3: 2})(
            totals, *sends
        )
    received = [across(s, shift) for shift, s in zip(SHIFTS, sends)]
    scaled, like = call(finish_kernel, (plane, shape((1, batch), F32)), "finish")(
        own, *received, totals, emit, prior, f1, g2, chain, part, length_row
    )
    return scaled, like.reshape(batch)


def solution(mesh):
    in_specs = (P("col", None), P(), P(), P(), P(), P(), P("col"), P(), P("grp", None), P("grp"))
    out_specs = (P("grp", "col"), P("grp"))
    return jax.shard_map(
        per_device, mesh=mesh, in_specs=in_specs, out_specs=out_specs, check_vma=False
    )
```
